128 devices in a mesh: segment: 4 (over y), blk: 32 (over z, x, core).
Axes of the slice: x: 4, y: 4, z: 4, core: 2. Of those that a mesh axis runs over, the one named last changes fastest.
Arguments:
- echoes: bfloat16 [4, 2048, 128, 512], P('segment', 'blk'), may hold values from -6 to 6
- train_blocks: int32 [4, 256, 6], P('segment', 'blk'), may hold values from 0 to 63, as said below
- hard_bins: int32 [4, 256], P('segment', 'blk'), may hold values 0 or 1
- owner_map: int32 [256], replicated, may hold values from 0 to 255, each once
- code_phase: float32 [64], replicated, may hold values from -3.140625 to 3.140625
Outputs:
- returns: bfloat16 [4, 256, 2048, 256], P('segment', 'blk')
The draws below stay inside these ranges and needn't reach their ends.
Inputs may be any that keep to these rules, and one draw needn't show every extreme that they name: `train_blocks`: each row lists 6 different training blocks.
All inputs are finite; a program needn't handle non-finite values. No bound on the sum of `hard_bins` on one device may be relied on, other than what follows from the above.
Results may differ from the reference program's by a relative error of at most 0.0086.
Values may be sent and summed in bfloat16 or wider, within the bound.
No kernel may reach another device: no remote copies, remote signals or barrier semaphores. Data moves between devices by JAX's collectives and lax.ppermute only.
A program may use at most 128 MiB of HBM per device.

```python
import math
import jax
import jax.numpy as jnp
from jax import lax

CH = 128
PULSES = 256
BEAMS = 128
RB = 32
NTR = 6
NTR_EASY = 3
NS_STEPS = 12
CBLK = 128
CODE_LEN = 64
BINS = 256
INTERVALS = 4
RANGES = 2048
NBLOCKS = 64


def draw_train_blocks(key, part):
    row_keys = jax.random.split(key, INTERVALS * BINS)

    def listing(row_key):
        return jax.random.permutation(row_key, NBLOCKS)[:NTR]
    listed = jax.vmap(listing)(row_keys)
    return listed.reshape(INTERVALS, BINS, NTR).astype(jnp.int32)


def with_ends(entries, rng, low, largest):
    shape = entries.shape
    place = [jax.random.randint(jax.random.fold_in(rng, axis), (), 0, shape[axis]) for axis in range(len(shape))]
    entries = entries.at[tuple(place)].set(low)
    longest = shape.index(max(shape))
    place[longest] = (place[longest] + 1) % shape[longest]
    return entries.at[tuple(place)].set(largest)


def block_scale(own_key, shape, pieces, least, top_value):
    def one(position, shards_of):
        draws = jax.random.uniform(jax.random.fold_in(jax.random.fold_in(own_key, 6), position), (shards_of,), jnp.float32, least / len(pieces), top_value / len(pieces))
        return jnp.repeat(jnp.exp(draws), shape[position] // shards_of).reshape((-1,) + (1,) * (len(shape) - position - 1))

    factor_of = one(*pieces[0])
    for cut in pieces[1:]:
        factor_of = factor_of * one(*cut)
    return factor_of


def scatter_about(key, shape, width, limit, pieces=(), held_as=jnp.bfloat16):
    result = jax.random.normal(key, shape, jnp.float32) * width
    if len(pieces) > 0:
        result = block_scale(key, shape, pieces, -0.22, 0.18) * result
    return jnp.clip(result, min=-limit, max=limit).astype(held_as)


def setup_inputs(seed: int = 0) -> dict:
    key_of = jax.random.split(jax.random.key(seed), 6)
    echoes = scatter_about(key_of[0], (INTERVALS, RANGES, CH, 2 * PULSES), 1.0, 6.0, ((0, 4), (1, 32)))
    train_blocks = draw_train_blocks(jax.random.fold_in(key_of[5], 71), 0)
    hard_bins = with_ends((jax.random.randint(key_of[2], (INTERVALS, BINS), 0, 4) < 1).astype(jnp.int32), jax.random.fold_in(key_of[2], 1), 0, 1)
    owner_map = jax.random.permutation(key_of[3], BINS).astype(jnp.int32)
    code_phase = jnp.clip(jax.random.uniform(key_of[4], (CODE_LEN,), jnp.float32, -3.140625, 3.140625), -3.140625, 3.140625)
    return dict(echoes=echoes, train_blocks=train_blocks, hard_bins=hard_bins, owner_map=owner_map, code_phase=code_phase)


decay_rate = 0.7
diag_load = 0.1
highest = lax.Precision.HIGHEST

def doppler_table(owner_map, pulse_count):
    pulse_index = jnp.arange(pulse_count, dtype=jnp.int32)
    phase_steps = pulse_index[:, None] * owner_map[None, :] % pulse_count
    angles = phase_steps.astype(jnp.float32) * (2.0 * math.pi / pulse_count)
    cosine = jnp.cos(angles) / math.sqrt(pulse_count)
    sine_part = jnp.sin(angles) / math.sqrt(pulse_count)
    real_rows = jnp.stack([cosine, -sine_part], axis=1)
    imag_rows = jnp.stack([sine_part, cosine], axis=1)
    return jnp.concatenate([real_rows, imag_rows], axis=0).astype(jnp.bfloat16)

def doppler(samples, dft_table):
    range_count, channels, _ = samples.shape
    spectra = jnp.einsum('rcp,pkj->jrkc', samples.astype(jnp.float32), dft_table.astype(jnp.float32))
    return spectra.astype(jnp.bfloat16).reshape(dft_table.shape[2], range_count, 2 * channels)

def covariance_half(spectra, blocks, hard, block_len, easy_count):
    bin_count, range_count, row_width = spectra.shape
    channels = row_width // 2
    listed = blocks.shape[1]
    blocked = spectra.reshape(bin_count, range_count // block_len, block_len, row_width)
    chosen = jnp.take_along_axis(blocked, blocks[:, :, None, None].astype(jnp.int32), axis=1)
    keep_mask = (jnp.arange(listed, dtype=jnp.int32)[None, :] < easy_count) | (hard[:, None] == 1)
    weighted = chosen * keep_mask[:, :, None, None].astype(jnp.bfloat16)
    train_rows = chosen.reshape(bin_count, listed * block_len, row_width)
    weighted = weighted.reshape(bin_count, listed * block_len, row_width)
    real_part = train_rows[..., :channels]
    imag_part = train_rows[..., channels:]
    left_side = jnp.concatenate([train_rows, jnp.concatenate([imag_part, -real_part], axis=-1)], axis=1)
    right_side = jnp.concatenate([weighted[..., :channels], weighted[..., channels:]], axis=1)
    gram_sum = jnp.einsum('nsf,nsg->nfg', left_side.astype(jnp.float32), right_side.astype(jnp.float32))
    row_count = jnp.where(hard == 1, listed * block_len, easy_count * block_len).astype(jnp.float32)
    return gram_sum / row_count[:, None, None]

def steering(channels, beams):
    channel_index = jnp.arange(channels, dtype=jnp.int32)
    beam_index = jnp.arange(beams, dtype=jnp.int32)
    phase_steps = channel_index[:, None] * (2 * beam_index[None, :] - beams) % (2 * beams)
    angles = phase_steps.astype(jnp.float32) * (math.pi / beams)
    return (jnp.cos(angles) / math.sqrt(channels), jnp.sin(angles) / math.sqrt(channels))

def complex_product(first_re, first_im, second_re, second_im):

    def matmul(first, second):
        return jnp.einsum('nij,njk->nik', first, second, precision=highest)
    return (matmul(first_re, second_re) - matmul(first_im, second_im), matmul(first_re, second_im) + matmul(first_im, second_re))

def beam_weights(cov_half, steer_re, steer_im, steps):
    channels = cov_half.shape[2]
    identity = jnp.eye(channels, dtype=jnp.float32)
    cov_re = cov_half[:, :channels] + diag_load * identity
    cov_im = cov_half[:, channels:]
    trace_value = jnp.trace(cov_re, axis1=1, axis2=2)
    start_re = identity[None] / trace_value[:, None, None]
    start_im = jnp.zeros_like(start_re)

    def newton(step_index, inverse_pair):
        inverse_re, inverse_im = inverse_pair
        middle_re, middle_im = complex_product(cov_re, cov_im, inverse_re, inverse_im)
        return complex_product(inverse_re, inverse_im, 2.0 * identity - middle_re, -middle_im)
    inverse_re, inverse_im = lax.fori_loop(0, steps, newton, (start_re, start_im))

    def apply(matrix, table):
        return jnp.einsum('nij,jb->nib', matrix, table, precision=highest)
    vec_re = apply(inverse_re, steer_re) - apply(inverse_im, steer_im)
    vec_im = apply(inverse_re, steer_im) + apply(inverse_im, steer_re)
    beam_gain = lax.optimization_barrier(jnp.sum(steer_re * vec_re + steer_im * vec_im, axis=1))
    weight_re = vec_re / beam_gain[:, None, :]
    weight_im = vec_im / beam_gain[:, None, :]
    upper_rows = jnp.concatenate([weight_re, -weight_im], axis=2)
    lower_rows = jnp.concatenate([weight_im, weight_re], axis=2)
    return jnp.concatenate([upper_rows, lower_rows], axis=1).astype(jnp.bfloat16)

def compression_table(code_phase, block_len):
    length = code_phase.shape[0]
    input_pos = jnp.arange(2 * block_len, dtype=jnp.int32)[:, None]
    output_pos = jnp.arange(block_len, dtype=jnp.int32)[None, :]
    lag_index = input_pos - output_pos
    onehot = (lag_index[:, :, None] == jnp.arange(length, dtype=jnp.int32)[None, None, :]).astype(jnp.float32)
    code_table = jnp.stack([jnp.cos(code_phase), jnp.sin(code_phase)]) / math.sqrt(length)
    table = jnp.einsum('qpl,kl->qkp', onehot, code_table, precision=highest)
    return table.astype(jnp.bfloat16)

def compress(formed, table, block_len):
    bin_count, range_count, row_width = formed.shape
    beam_half = row_width // 2
    blocks = formed.reshape(bin_count, range_count // block_len, block_len, row_width)
    next_blocks = jnp.concatenate([blocks[:, 1:], jnp.zeros_like(blocks[:, :1])], axis=1)
    paired = jnp.concatenate([blocks, next_blocks], axis=2)
    mixed_terms = jnp.einsum('nbqe,qkp->nbkpe', paired.astype(jnp.float32), table.astype(jnp.float32))
    result_re = mixed_terms[:, :, 0, :, :beam_half] + mixed_terms[:, :, 1, :, beam_half:]
    result_im = mixed_terms[:, :, 0, :, beam_half:] - mixed_terms[:, :, 1, :, :beam_half]
    joined = jnp.concatenate([result_re, result_im], axis=-1)
    return joined.reshape(bin_count, range_count, row_width).astype(jnp.bfloat16)

def reference(echoes, train_blocks, hard_bins, owner_map, code_phase):
    dft_table = doppler_table(owner_map, PULSES)
    steer_re, steer_im = steering(CH, BEAMS)
    comp_table = compression_table(code_phase, CBLK)
    spectra_list = []
    cov_list = []
    for interval in range(INTERVALS):
        spectra = doppler(echoes[interval], dft_table)
        spectra_list.append(spectra)
        cov_list.append(covariance_half(spectra, train_blocks[interval], hard_bins[interval], RB, NTR_EASY))
    carried = jnp.zeros_like(cov_list[0])
    outputs = []
    for interval in range(INTERVALS):
        weights = beam_weights(carried, steer_re, steer_im, NS_STEPS)
        formed = jnp.einsum('nrf,nfe->nre', spectra_list[interval].astype(jnp.float32), weights.astype(jnp.float32)).astype(jnp.bfloat16)
        outputs.append(compress(formed, comp_table, CBLK))
        carried = decay_rate * carried + cov_list[interval]
    return jnp.stack(outputs)
```

```python
import math

import jax
import jax.numpy as jnp
from jax import lax
from jax.experimental import pallas as pl
from jax.experimental.pallas import tpu as pltpu
from jax.sharding import PartitionSpec as P


CH = 128
BEAMS = 128
RB = 32
NTR_EASY = 3
NS_STEPS = 12
CBLK = 128
CHUNKS = (3, 3, 2)

decay_rate = 0.7
diag_load = 0.1
highest = lax.Precision.HIGHEST
f32 = jnp.float32
bf16 = jnp.bfloat16
MiB = 1 << 20


def params(limit=48):
    return pltpu.CompilerParams(vmem_limit_bytes=limit * MiB)


def shifted(x, by):
    peers = lax.axis_size("segment")
    return lax.ppermute(x, "segment", [(i, i + by) for i in range(peers - by)])


def unit_phasor(index, period):
    eighth = period // 8
    turned = index + eighth
    quadrant = lax.shift_right_logical(turned, int(math.log2(period // 4))) & 3
    rest = (turned & (period // 4 - 1)) - eighth
    x = rest.astype(f32) * (2.0 * math.pi / period)
    x2 = x * x
    sine = x + x * x2 * (-1.0 / 6 + x2 * (1.0 / 120 + x2 * (-1.0 / 5040 + x2 * (1.0 / 362880))))
    cosine = 1.0 + x2 * (
        -0.5 + x2 * (1.0 / 24 + x2 * (-1.0 / 720 + x2 * (1.0 / 40320 - x2 * (1.0 / 3628800))))
    )
    swap = (quadrant & 1) == 1
    c = jnp.where(swap, sine, cosine)
    s = jnp.where(swap, cosine, sine)
    c = jnp.where((quadrant == 1) | (quadrant == 2), -c, c)
    s = jnp.where(quadrant >= 2, -s, s)
    return c, s


def doppler_kernel(map_ref, x_ref, o_ref, table_ref, rows_ref):
    slots, rows, _ = o_ref.shape
    pulses = x_ref.shape[2] // 2

    @pl.when(pl.program_id(0) == 0)
    def _():
        pulse = lax.broadcasted_iota(jnp.int32, (slots, pulses), 1)
        c, s = unit_phasor((pulse * map_ref[...]) & (pulses - 1), pulses)
        c = (c * (1.0 / math.sqrt(pulses))).astype(bf16)
        s = (s * (1.0 / math.sqrt(pulses))).astype(bf16)
        table_ref[:slots, :pulses] = c
        table_ref[:slots, pulses:] = s
        table_ref[slots:, :pulses] = -s
        table_ref[slots:, pulses:] = c

    for pair in range(rows // 2):
        x = x_ref[2 * pair : 2 * pair + 2].reshape(2 * CH, 2 * pulses)
        d = lax.dot_general(
            table_ref[...], x, (((1,), (1,)), ((), ())), preferred_element_type=f32
        )
        for part in range(2):
            for half in range(2):
                rows_ref[part, pl.ds(2 * pair + half, slots, stride=rows), :] = d[
                    part * slots : (part + 1) * slots, half * CH : (half + 1) * CH
                ]
    for part in range(2):
        o_ref[:, :, part * CH : (part + 1) * CH] = (
            rows_ref[part].reshape(slots, rows, CH).astype(bf16)
        )


def doppler(samples, bins):
    range_local, channels, double_pulses = samples.shape
    slots = bins.shape[0]
    step = 16
    return pl.pallas_call(
        doppler_kernel,
        out_shape=pltpu.HBM((slots, range_local, 2 * channels), bf16),
        grid=(range_local // step,),
        in_specs=[
            pl.BlockSpec((slots, 1), lambda i: (0, 0)),
            pl.BlockSpec((step, channels, double_pulses), lambda i: (i, 0, 0)),
        ],
        out_specs=pl.BlockSpec((slots, step, 2 * channels), lambda i: (0, i, 0)),
        scratch_shapes=[
            pltpu.VMEM((2 * slots, double_pulses), bf16),
            pltpu.VMEM((2, slots * step, channels), f32),
        ],
        compiler_params=pltpu.CompilerParams(vmem_limit_bytes=67_043_328),
        name="doppler",
    )(bins, samples)


def make_cov_kernel(first, count, listed):
    def cov_kernel(blocks_ref, hard_ref, y_ref, o_ref, buf, sem):
        per_source = y_ref.shape[2] // RB

        def copy(i, t):
            block = blocks_ref[(first + i) * listed + t]
            source = block // per_source
            row = pl.multiple_of((block % per_source) * RB, RB)
            return pltpu.make_async_copy(
                y_ref.at[source, i, pl.ds(row, RB), :], buf.at[i, t], sem.at[i, t]
            )

        for i in range(count):
            for t in range(listed):
                copy(i, t).start()
        row_of = lax.broadcasted_iota(jnp.int32, (listed * RB, 1), 0)
        f = lax.broadcasted_iota(jnp.int32, (CH, CH), 0)
        g = lax.broadcasted_iota(jnp.int32, (CH, CH), 1)
        for i in range(count):
            for t in range(listed):
                copy(i, t).wait()
            hard = hard_ref[first + i] == 1
            used = jnp.where(hard, listed * RB, NTR_EASY * RB)
            mask = (row_of < used).astype(f32).astype(bf16)
            y = buf[i].reshape(listed * RB, 2 * CH) * mask
            gram = lax.dot_general(y, y, (((0,), (0,)), ((), ())), preferred_element_type=f32)
            re = gram[:CH, :CH] + gram[CH:, CH:]
            im = gram[CH:, :CH] - gram[:CH, CH:]
            o_ref[i] = jnp.where(f <= g, re, im) / used.astype(f32)

    return cov_kernel


def covariance(owned, blocks, hard, first):
    count = owned.shape[1]
    listed = blocks.shape[1]
    smem = pl.BlockSpec(memory_space=pltpu.SMEM)
    return pl.pallas_call(
        make_cov_kernel(first, count, listed),
        out_shape=jax.ShapeDtypeStruct((count, CH, CH), f32),
        in_specs=[smem, smem, pl.BlockSpec(memory_space=pltpu.HBM)],
        out_specs=pl.BlockSpec(memory_space=pltpu.VMEM),
        scratch_shapes=[
            pltpu.VMEM((count, listed, RB, 2 * CH), bf16),
            pltpu.SemaphoreType.DMA((count, listed)),
        ],
        compiler_params=params(),
        name="covariance",
    )(blocks.reshape(-1), hard, owned)


def halves(z):
    high = z.astype(bf16)
    return high, (z - high.astype(f32)).astype(bf16)


def left(z):
    high, low = halves(z)
    return jnp.concatenate([high, low, high], axis=1)


def right(z):
    high, low = halves(z)

    def real_form(x):
        return jnp.concatenate([x, jnp.concatenate([-x[:, CH:], x[:, :CH]], axis=1)], axis=0)

    big = real_form(high)
    return jnp.concatenate([big, big, real_form(low)], axis=0)


def times(a, b):
    return jnp.dot(left(a), right(b), preferred_element_type=f32)


def weights_kernel(c1_ref, c2_ref, c3_ref, o_ref, x_ref, a_ref):
    count = o_ref.shape[0]
    f = lax.broadcasted_iota(jnp.int32, (CH, CH), 0)
    g = lax.broadcasted_iota(jnp.int32, (CH, CH), 1)
    eye = (f == g).astype(f32)
    eye2 = jnp.concatenate([eye, jnp.zeros_like(eye)], axis=1)
    rows = lambda z, k: z[k * CH : (k + 1) * CH]
    for i in range(count):
        packed = c1_ref[i] + decay_rate * c2_ref[i] + (decay_rate * decay_rate) * c3_ref[i]
        flipped = packed.T
        re = jnp.where(f <= g, packed, flipped) + diag_load * eye
        im = jnp.where(f > g, packed, jnp.where(f < g, -flipped, 0.0))
        trace = jnp.sum(jnp.sum(re * eye, axis=1, keepdims=True), axis=0, keepdims=True)
        scale = 1.0 / trace
        a = jnp.concatenate([re, im], axis=1)
        a_ref[i] = right(a)
        e = eye2 - a * scale
        x = (eye2 + e) * scale
        e = times(e, e)
        both = jnp.dot(left(jnp.concatenate([x, e], axis=0)), right(e), preferred_element_type=f32)
        x = x + rows(both, 0)
        x_ref[i] = x + times(x, rows(both, 1))

    def three(_, carry):
        for i in range(count):
            x = x_ref[i]
            e = eye2 - jnp.dot(left(x), a_ref[i], preferred_element_type=f32)
            for _ in range(2):
                both = jnp.dot(
                    left(jnp.concatenate([x, e], axis=0)), right(e), preferred_element_type=f32
                )
                x = x + rows(both, 0)
                e = rows(both, 1)
            x_ref[i] = x + times(x, e)
        return carry

    lax.fori_loop(0, NS_STEPS // 3 - 1, three, 0)
    c, s = unit_phasor((f * (2 * g - BEAMS)) & (2 * BEAMS - 1), 2 * BEAMS)
    steer = jnp.concatenate([c, s], axis=1) * (1.0 / math.sqrt(CH))
    table = right(steer)
    for i in range(count):
        vec = jnp.dot(left(x_ref[i]), table, preferred_element_type=f32)
        both = steer * vec
        gain = jnp.sum(both[:, :BEAMS] + both[:, BEAMS:], axis=0, keepdims=True)
        re = (vec[:, :BEAMS] / gain).astype(bf16)
        im = (vec[:, BEAMS:] / gain).astype(bf16)
        o_ref[i, :CH, :BEAMS] = re
        o_ref[i, :CH, BEAMS:] = -im
        o_ref[i, CH:, :BEAMS] = im
        o_ref[i, CH:, BEAMS:] = re


def beam_weights(c1, c2, c3):
    count = c1.shape[0]
    vmem = pl.BlockSpec(memory_space=pltpu.VMEM)
    return pl.pallas_call(
        weights_kernel,
        out_shape=jax.ShapeDtypeStruct((count, 2 * CH, 2 * BEAMS), bf16),
        in_specs=[vmem] * 3,
        out_specs=vmem,
        scratch_shapes=[
            pltpu.VMEM((count, CH, 2 * CH), f32),
            pltpu.VMEM((count, 6 * CH, 2 * CH), bf16),
        ],
        compiler_params=params(),
        name="weights",
    )(c1, c2, c3)


def compression_table(code_phase, block_len):
    length = code_phase.shape[0]
    input_pos = jnp.arange(2 * block_len, dtype=jnp.int32)[None, :]
    output_pos = jnp.arange(block_len, dtype=jnp.int32)[:, None]
    lag_index = input_pos - output_pos
    onehot = (lag_index[:, :, None] == jnp.arange(length, dtype=jnp.int32)[None, None, :]).astype(
        jnp.float32
    )
    code_table = jnp.stack([jnp.cos(code_phase), jnp.sin(code_phase)]) / math.sqrt(length)
    table = jnp.einsum("pql,kl->kpq", onehot, code_table, precision=highest)
    return table.astype(bf16).reshape(2 * block_len, 2 * block_len)


def compress_kernel(table_ref, y_ref, o_ref):
    per = y_ref.shape[2]
    step = CBLK // per
    sources = y_ref.shape[0]
    half = CH
    for start in range(0, sources, step):
        stop = min(start + 2 * step, sources)
        y = y_ref[start:stop, 0].reshape((stop - start) * per, 2 * half)
        if stop - start < 2 * step:
            y = jnp.concatenate([y, jnp.zeros_like(y)], axis=0)
        m = jnp.dot(table_ref[...], y, preferred_element_type=f32)
        r = pl.ds(start * per, CBLK)
        o_ref[0, r, :half] = (m[:CBLK, :half] + m[CBLK:, half:]).astype(bf16)
        o_ref[0, r, half:] = (m[:CBLK, half:] - m[CBLK:, :half]).astype(bf16)


def compress(owned, table):
    sources, count, per, width = owned.shape
    return pl.pallas_call(
        compress_kernel,
        out_shape=jax.ShapeDtypeStruct((count, sources * per, width), bf16),
        grid=(count,),
        in_specs=[
            pl.BlockSpec(table.shape, lambda i: (0, 0)),
            pl.BlockSpec((sources, 1, per, width), lambda i: (0, i, 0, 0)),
        ],
        out_specs=pl.BlockSpec((1, sources * per, width), lambda i: (i, 0, 0)),
        compiler_params=params(),
        name="compress",
    )(table, owned)


def beams_kernel(w_ref, z_ref, *refs):
    o_ref = refs[-1]
    o_ref[0] = jnp.dot(z_ref[0], w_ref[0], preferred_element_type=f32).astype(bf16)


def form_beams(z, weights, held, bins, first):
    count, rows, width = z.shape
    step = rows // 2
    in_specs = [
        pl.BlockSpec((1, width, weights.shape[2]), lambda i, h: (i, 0, 0)),
        pl.BlockSpec((1, step, width), lambda i, h: (i, h, 0)),
    ]
    operands = [weights, z]
    aliases = {}
    if held is not None:
        in_specs.append(pl.BlockSpec(memory_space=pl.ANY))
        operands.append(held)
        aliases = {2: 0}
    return pl.pallas_call(
        beams_kernel,
        out_shape=jax.ShapeDtypeStruct((bins, rows, weights.shape[2]), bf16),
        grid=(count, 2),
        in_specs=in_specs,
        out_specs=pl.BlockSpec((1, step, weights.shape[2]), lambda i, h: (first + i, h, 0)),
        input_output_aliases=aliases,
        compiler_params=params(),
        name="beams",
    )(*operands)


def chain(echoes, train_blocks, hard_bins, owner_map, code_phase):
    samples = echoes[0]
    blocks, hard = train_blocks[0], hard_bins[0]
    owners = lax.axis_size("blk")
    bins = hard.shape[0]
    slot_bins = owner_map.reshape(owners, bins)
    firsts = [sum(CHUNKS[:i]) for i in range(len(CHUNKS))]
    spectra = []
    for first, count in zip(firsts, CHUNKS):
        chosen = slot_bins[:, first : first + count].reshape(-1, 1)
        spectra.append(doppler(samples, chosen).reshape(owners, count, samples.shape[0], 2 * CH))
    code_phase, spectra[0] = lax.optimization_barrier((code_phase, spectra[0]))
    table = compression_table(code_phase, CBLK)
    owned = []
    for g, sent in enumerate(spectra):
        if g > 0:
            sent, owned[-1] = lax.optimization_barrier((sent, owned[-1]))
        owned.append(lax.all_to_all(sent, "blk", split_axis=0, concat_axis=0, tiled=True))
    result = None
    for first, y in zip(firsts, owned):
        if result is not None:
            y, result = lax.optimization_barrier((y, result))
        cov = covariance(y, blocks, hard, first)
        c1, c2, c3 = shifted(cov, 1), shifted(cov, 2), shifted(cov, 3)
        z = compress(y, table)
        weights = beam_weights(c1, c2, c3)
        result = form_beams(z, weights, result, bins, first)
    return result[None]


def solution(mesh):
    in_specs = (
        P("segment", "blk", None, None),
        P("segment", "blk", None),
        P("segment", "blk"),
        P(),
        P(),
    )
    out_specs = P("segment", "blk", None, None)
    return jax.shard_map(chain, mesh=mesh, in_specs=in_specs, out_specs=out_specs, check_vma=False)
```

```python
import math

import jax
import jax.numpy as jnp
from jax import lax
from jax.experimental import pallas as pl
from jax.experimental.pallas import tpu as pltpu
from jax.sharding import PartitionSpec as P


CH = 128
BEAMS = 128
RB = 32
NTR_EASY = 3
NS_STEPS = 12
CBLK = 128
CHUNKS = (3, 3, 2)

decay_rate = 0.7
diag_load = 0.1
highest = lax.Precision.HIGHEST
f32 = jnp.float32
bf16 = jnp.bfloat16
MiB = 1 << 20


def params(limit=48):
    return pltpu.CompilerParams(vmem_limit_bytes=limit * MiB)


def shifted(x, by):
    peers = lax.axis_size("segment")
    return lax.ppermute(x, "segment", [(i, (i + by) % peers) for i in range(peers)])


def unit_phasor(index, period):
    eighth = period // 8
    turned = index + eighth
    quadrant = lax.shift_right_logical(turned, int(math.log2(period // 4))) & 3
    rest = (turned & (period // 4 - 1)) - eighth
    x = rest.astype(f32) * (2.0 * math.pi / period)
    x2 = x * x
    sine = x + x * x2 * (-1.0 / 6 + x2 * (1.0 / 120 + x2 * (-1.0 / 5040 + x2 * (1.0 / 362880))))
    cosine = 1.0 + x2 * (
        -0.5 + x2 * (1.0 / 24 + x2 * (-1.0 / 720 + x2 * (1.0 / 40320 - x2 * (1.0 / 3628800))))
    )
    swap = (quadrant & 1) == 1
    c = jnp.where(swap, sine, cosine)
    s = jnp.where(swap, cosine, sine)
    c = jnp.where((quadrant == 1) | (quadrant == 2), -c, c)
    s = jnp.where(quadrant >= 2, -s, s)
    return c, s


def make_doppler_kernel(owners, first, count):
    def doppler_kernel(map_ref, x_hbm, o_hbm, x_ref, table_ref, rows_ref, o_ref, in_sem, out_sem):
        slots = owners * count
        total = map_ref.shape[1]
        bins = total // owners
        pulses = x_ref.shape[2] // 2
        groups, _, rows, _ = o_ref.shape
        pitch = rows_ref.shape[1] // slots
        loads = in_sem.shape[0]
        per_load = x_ref.shape[0] // loads

        def load(i):
            piece = pl.ds(i * per_load, per_load)
            return pltpu.make_async_copy(x_hbm.at[piece], x_ref.at[piece], in_sem.at[i])

        def save(i):
            piece = o_hbm.at[:, pl.ds(i * rows, rows), :]
            return pltpu.make_async_copy(o_ref.at[i], piece, out_sem.at[i])

        for i in range(loads):
            load(i).start()
        slot = lax.broadcasted_iota(jnp.int32, (slots, total), 1)
        row = lax.broadcasted_iota(jnp.int32, (slots, total), 0)
        place = slot % bins - first
        mine = (place >= 0) & (place < count) & (slot // bins * count + place == row)
        chosen = jnp.sum(jnp.where(mine, map_ref[...].astype(f32), 0.0), axis=1, keepdims=True)
        pulse = lax.broadcasted_iota(jnp.int32, (slots, pulses), 1)
        c, s = unit_phasor((pulse * chosen.astype(jnp.int32)) & (pulses - 1), pulses)
        c = (c * (1.0 / math.sqrt(pulses))).astype(bf16)
        s = (s * (1.0 / math.sqrt(pulses))).astype(bf16)
        table_ref[:slots, :pulses] = c
        table_ref[:slots, pulses:] = s
        table_ref[slots:, :pulses] = -s
        table_ref[slots:, pulses:] = c

        def group(i, carry):
            for j in range(loads // groups):
                load(i * (loads // groups) + j).wait()
            for pair in range(rows // 2):
                x = x_ref[pl.ds(i * rows + 2 * pair, 2)].reshape(2 * CH, 2 * pulses)
                d = lax.dot_general(
                    table_ref[...], x, (((1,), (1,)), ((), ())), preferred_element_type=f32
                )
                for part in range(2):
                    for half in range(2):
                        rows_ref[part, pl.ds(2 * pair + half, slots, stride=pitch), :] = d[
                            part * slots : (part + 1) * slots, half * CH : (half + 1) * CH
                        ]
            for part in range(2):
                o_ref[i, :, :, part * CH : (part + 1) * CH] = (
                    rows_ref[part].reshape(slots, pitch, CH)[:, :rows].astype(bf16)
                )
            save(i).start()
            return carry

        lax.fori_loop(0, groups, group, 0)
        for i in range(groups):
            save(i).wait()

    return doppler_kernel


def doppler(samples, owner_map, owners, first, count):
    range_local, channels, double_pulses = samples.shape
    slots = owners * count
    rows, pitch, loads = 16, 24, 8
    groups = range_local // rows
    return pl.pallas_call(
        make_doppler_kernel(owners, first, count),
        out_shape=pltpu.HBM((slots, range_local, 2 * channels), bf16),
        in_specs=[
            pl.BlockSpec(memory_space=pltpu.VMEM),
            pl.BlockSpec(memory_space=pl.ANY),
        ],
        out_specs=pl.BlockSpec(memory_space=pl.ANY),
        scratch_shapes=[
            pltpu.VMEM(samples.shape, bf16),
            pltpu.VMEM((2 * slots, double_pulses), bf16),
            pltpu.VMEM((2, slots * pitch, channels), f32),
            pltpu.VMEM((groups, slots, rows, 2 * channels), bf16),
            pltpu.SemaphoreType.DMA((loads,)),
            pltpu.SemaphoreType.DMA((groups,)),
        ],
        compiler_params=pltpu.CompilerParams(vmem_limit_bytes=67_043_328),
        name="doppler",
    )(owner_map.reshape(1, -1), samples)


def make_cov_kernel(first, count, listed):
    def cov_kernel(blocks_ref, hard_ref, y_ref, o_ref, buf, sem):
        per_source = y_ref.shape[2] // RB

        def copy(i, t):
            block = blocks_ref[first + i, t]
            source = block // per_source
            row = pl.multiple_of((block % per_source) * RB, RB)
            return pltpu.make_async_copy(
                y_ref.at[source, i, pl.ds(row, RB), :], buf.at[i, t], sem.at[i, t]
            )

        for i in range(count):
            for t in range(listed):
                copy(i, t).start()
        row_of = lax.broadcasted_iota(jnp.int32, (listed * RB, 1), 0)
        f = lax.broadcasted_iota(jnp.int32, (CH, CH), 0)
        g = lax.broadcasted_iota(jnp.int32, (CH, CH), 1)
        for i in range(count):
            for t in range(listed):
                copy(i, t).wait()
            hard = hard_ref[first + i] == 1
            used = jnp.where(hard, listed * RB, NTR_EASY * RB)
            mask = (row_of < used).astype(f32).astype(bf16)
            y = buf[i].reshape(listed * RB, 2 * CH) * mask
            gram = lax.dot_general(y, y, (((0,), (0,)), ((), ())), preferred_element_type=f32)
            re = gram[:CH, :CH] + gram[CH:, CH:]
            im = gram[CH:, :CH] - gram[:CH, CH:]
            o_ref[i] = jnp.where(f <= g, re, im) / used.astype(f32)

    return cov_kernel


def covariance(owned, blocks, hard, first):
    count = owned.shape[1]
    listed = blocks.shape[1]
    smem = pl.BlockSpec(memory_space=pltpu.SMEM)
    return pl.pallas_call(
        make_cov_kernel(first, count, listed),
        out_shape=jax.ShapeDtypeStruct((count, CH, CH), f32),
        in_specs=[smem, smem, pl.BlockSpec(memory_space=pltpu.HBM)],
        out_specs=pl.BlockSpec(memory_space=pltpu.VMEM),
        scratch_shapes=[
            pltpu.VMEM((count, listed, RB, 2 * CH), bf16),
            pltpu.SemaphoreType.DMA((count, listed)),
        ],
        compiler_params=params(),
        name="covariance",
    )(blocks, hard, owned)


def halves(z):
    high = z.astype(bf16)
    return high, (z - high.astype(f32)).astype(bf16)


def left(z):
    high, low = halves(z)
    return jnp.concatenate([high, low, high], axis=1)


def right(z):
    high, low = halves(z)

    def real_form(x):
        return jnp.concatenate([x, jnp.concatenate([-x[:, CH:], x[:, :CH]], axis=1)], axis=0)

    big = real_form(high)
    return jnp.concatenate([big, big, real_form(low)], axis=0)


def times(a, b):
    return jnp.dot(left(a), right(b), preferred_element_type=f32)


def weights_kernel(c1_ref, c2_ref, c3_ref, o_ref, x_ref, a_ref):
    count = o_ref.shape[0]
    f = lax.broadcasted_iota(jnp.int32, (CH, CH), 0)
    g = lax.broadcasted_iota(jnp.int32, (CH, CH), 1)
    eye = (f == g).astype(f32)
    eye2 = jnp.concatenate([eye, jnp.zeros_like(eye)], axis=1)
    rows = lambda z, k: z[k * CH : (k + 1) * CH]
    segment = lax.axis_index("segment")
    decay = [jnp.where(segment > n, decay_rate**n, 0.0) for n in range(3)]
    for i in range(count):
        packed = decay[0] * c1_ref[i] + decay[1] * c2_ref[i] + decay[2] * c3_ref[i]
        flipped = packed.T
        re = jnp.where(f <= g, packed, flipped) + diag_load * eye
        im = jnp.where(f > g, packed, jnp.where(f < g, -flipped, 0.0))
        trace = jnp.sum(jnp.sum(re * eye, axis=1, keepdims=True), axis=0, keepdims=True)
        scale = 1.0 / trace
        a = jnp.concatenate([re, im], axis=1)
        a_ref[i] = right(a)
        e = eye2 - a * scale
        x = (eye2 + e) * scale
        e = times(e, e)
        both = jnp.dot(left(jnp.concatenate([x, e], axis=0)), right(e), preferred_element_type=f32)
        x = x + rows(both, 0)
        x_ref[i] = x + times(x, rows(both, 1))

    def three(_, carry):
        for i in range(count):
            x = x_ref[i]
            e = eye2 - jnp.dot(left(x), a_ref[i], preferred_element_type=f32)
            for _ in range(2):
                both = jnp.dot(
                    left(jnp.concatenate([x, e], axis=0)), right(e), preferred_element_type=f32
                )
                x = x + rows(both, 0)
                e = rows(both, 1)
            x_ref[i] = x + times(x, e)
        return carry

    lax.fori_loop(0, NS_STEPS // 3 - 1, three, 0)
    c, s = unit_phasor((f * (2 * g - BEAMS)) & (2 * BEAMS - 1), 2 * BEAMS)
    steer = jnp.concatenate([c, s], axis=1) * (1.0 / math.sqrt(CH))
    table = right(steer)
    for i in range(count):
        vec = jnp.dot(left(x_ref[i]), table, preferred_element_type=f32)
        both = steer * vec
        gain = jnp.sum(both[:, :BEAMS] + both[:, BEAMS:], axis=0, keepdims=True)
        re = (vec[:, :BEAMS] / gain).astype(bf16)
        im = (vec[:, BEAMS:] / gain).astype(bf16)
        o_ref[i, :CH, :BEAMS] = re
        o_ref[i, :CH, BEAMS:] = -im
        o_ref[i, CH:, :BEAMS] = im
        o_ref[i, CH:, BEAMS:] = re


def beam_weights(c1, c2, c3):
    count = c1.shape[0]
    vmem = pl.BlockSpec(memory_space=pltpu.VMEM)
    return pl.pallas_call(
        weights_kernel,
        out_shape=jax.ShapeDtypeStruct((count, 2 * CH, 2 * BEAMS), bf16),
        in_specs=[vmem] * 3,
        out_specs=vmem,
        scratch_shapes=[
            pltpu.VMEM((count, CH, 2 * CH), f32),
            pltpu.VMEM((count, 6 * CH, 2 * CH), bf16),
        ],
        compiler_params=params(),
        name="weights",
    )(c1, c2, c3)


def compression_table(code_phase, block_len):
    length = code_phase.shape[0]
    input_pos = jnp.arange(2 * block_len, dtype=jnp.int32)[None, :]
    output_pos = jnp.arange(block_len, dtype=jnp.int32)[:, None]
    lag_index = input_pos - output_pos
    onehot = (lag_index[:, :, None] == jnp.arange(length, dtype=jnp.int32)[None, None, :]).astype(
        jnp.float32
    )
    code_table = jnp.stack([jnp.cos(code_phase), jnp.sin(code_phase)]) / math.sqrt(length)
    table = jnp.einsum("pql,kl->kpq", onehot, code_table, precision=highest)
    return table.astype(bf16).reshape(2 * block_len, 2 * block_len)


def compress_kernel(table_ref, y_ref, o_ref):
    per = y_ref.shape[2]
    step = CBLK // per
    sources = y_ref.shape[0]
    half = CH
    for start in range(0, sources, step):
        stop = min(start + 2 * step, sources)
        y = y_ref[start:stop, 0].reshape((stop - start) * per, 2 * half)
        if stop - start < 2 * step:
            y = jnp.concatenate([y, jnp.zeros_like(y)], axis=0)
        m = jnp.dot(table_ref[...], y, preferred_element_type=f32)
        r = pl.ds(start * per, CBLK)
        o_ref[0, r, :half] = (m[:CBLK, :half] + m[CBLK:, half:]).astype(bf16)
        o_ref[0, r, half:] = (m[:CBLK, half:] - m[CBLK:, :half]).astype(bf16)


def compress(owned, table):
    sources, count, per, width = owned.shape
    return pl.pallas_call(
        compress_kernel,
        out_shape=jax.ShapeDtypeStruct((count, sources * per, width), bf16),
        grid=(count,),
        in_specs=[
            pl.BlockSpec(table.shape, lambda i: (0, 0)),
            pl.BlockSpec((sources, 1, per, width), lambda i: (0, i, 0, 0)),
        ],
        out_specs=pl.BlockSpec((1, sources * per, width), lambda i: (i, 0, 0)),
        compiler_params=params(),
        name="compress",
    )(table, owned)


def beams_kernel(w_ref, z_ref, *refs):
    o_ref = refs[-1]
    o_ref[0] = jnp.dot(z_ref[0], w_ref[0], preferred_element_type=f32).astype(bf16)


def form_beams(z, weights, held, bins, first):
    count, rows, width = z.shape
    step = rows // 2
    in_specs = [
        pl.BlockSpec((1, width, weights.shape[2]), lambda i, h: (i, 0, 0)),
        pl.BlockSpec((1, step, width), lambda i, h: (i, h, 0)),
    ]
    operands = [weights, z]
    aliases = {}
    if held is not None:
        in_specs.append(pl.BlockSpec(memory_space=pl.ANY))
        operands.append(held)
        aliases = {2: 0}
    return pl.pallas_call(
        beams_kernel,
        out_shape=jax.ShapeDtypeStruct((bins, rows, weights.shape[2]), bf16),
        grid=(count, 2),
        in_specs=in_specs,
        out_specs=pl.BlockSpec((1, step, weights.shape[2]), lambda i, h: (first + i, h, 0)),
        input_output_aliases=aliases,
        compiler_params=params(),
        name="beams",
    )(*operands)


def chain(echoes, train_blocks, hard_bins, owner_map, code_phase):
    samples = echoes[0]
    blocks, hard = train_blocks[0], hard_bins[0]
    owners = lax.axis_size("blk")
    bins = hard.shape[0]
    firsts = [sum(CHUNKS[:i]) for i in range(len(CHUNKS))]
    spectra = []
    for first, count in zip(firsts, CHUNKS):
        sent = doppler(samples, owner_map, owners, first, count)
        spectra.append(sent.reshape(owners, count, samples.shape[0], 2 * CH))
    code_phase, spectra[0] = lax.optimization_barrier((code_phase, spectra[0]))
    table = compression_table(code_phase, CBLK)
    owned = []
    for g, sent in enumerate(spectra):
        if g > 0:
            sent, owned[-1] = lax.optimization_barrier((sent, owned[-1]))
        owned.append(lax.all_to_all(sent, "blk", split_axis=0, concat_axis=0, tiled=True))
    result = None
    for first, y in zip(firsts, owned):
        if result is not None:
            y, result = lax.optimization_barrier((y, result))
        cov = covariance(y, blocks, hard, first)
        c3, c1, c2 = shifted(cov, 3), shifted(cov, 1), shifted(cov, 2)
        z = compress(y, table)
        weights = beam_weights(c1, c2, c3)
        result = form_beams(z, weights, result, bins, first)
    return result[None]


def solution(mesh):
    in_specs = (
        P("segment", "blk", None, None),
        P("segment", "blk", None),
        P("segment", "blk"),
        P(),
        P(),
    )
    out_specs = P("segment", "blk", None, None)
    return jax.shard_map(chain, mesh=mesh, in_specs=in_specs, out_specs=out_specs, check_vma=False)
```

```python
import math

import jax
import jax.numpy as jnp
from jax import lax
from jax.experimental import pallas as pl
from jax.experimental.pallas import tpu as pltpu
from jax.sharding import PartitionSpec as P


CH = 128
BEAMS = 128
RB = 32
NTR_EASY = 3
NS_STEPS = 12
CBLK = 128
CHUNKS = (6, 2)

decay_rate = 0.7
diag_load = 0.1
highest = lax.Precision.HIGHEST
f32 = jnp.float32
bf16 = jnp.bfloat16
MiB = 1 << 20


def params(limit=48):
    return pltpu.CompilerParams(vmem_limit_bytes=limit * MiB)


def shifted(x, by):
    peers = lax.axis_size("segment")
    return lax.ppermute(x, "segment", [(i, (i + by) % peers) for i in range(peers)])


def unit_phasor(index, period):
    eighth = period // 8
    turned = index + eighth
    quadrant = lax.shift_right_logical(turned, int(math.log2(period // 4))) & 3
    rest = (turned & (period // 4 - 1)) - eighth
    x = rest.astype(f32) * (2.0 * math.pi / period)
    x2 = x * x
    sine = x + x * x2 * (-1.0 / 6 + x2 * (1.0 / 120 + x2 * (-1.0 / 5040 + x2 * (1.0 / 362880))))
    cosine = 1.0 + x2 * (
        -0.5 + x2 * (1.0 / 24 + x2 * (-1.0 / 720 + x2 * (1.0 / 40320 - x2 * (1.0 / 3628800))))
    )
    swap = (quadrant & 1) == 1
    c = jnp.where(swap, sine, cosine)
    s = jnp.where(swap, cosine, sine)
    c = jnp.where((quadrant == 1) | (quadrant == 2), -c, c)
    s = jnp.where(quadrant >= 2, -s, s)
    return c, s


def make_doppler_kernel(owners, first, count):
    def doppler_kernel(map_ref, x_hbm, o_hbm, x_ref, table_ref, rows_ref, o_ref, in_sem, out_sem):
        slots = owners * count
        total = map_ref.shape[1]
        bins = total // owners
        pulses = x_ref.shape[2] // 2
        groups, _, rows, _ = o_ref.shape
        pitch = rows_ref.shape[1] // slots
        loads = in_sem.shape[0]
        per_load = x_ref.shape[0] // loads

        def load(i):
            piece = pl.ds(i * per_load, per_load)
            return pltpu.make_async_copy(x_hbm.at[piece], x_ref.at[piece], in_sem.at[i])

        def save(i):
            piece = o_hbm.at[:, pl.ds(i * rows, rows), :]
            return pltpu.make_async_copy(o_ref.at[i], piece, out_sem.at[i])

        for i in range(loads):
            load(i).start()
        slot = lax.broadcasted_iota(jnp.int32, (slots, total), 1)
        row = lax.broadcasted_iota(jnp.int32, (slots, total), 0)
        place = slot % bins - first
        mine = (place >= 0) & (place < count) & (slot // bins * count + place == row)
        chosen = jnp.sum(jnp.where(mine, map_ref[...].astype(f32), 0.0), axis=1, keepdims=True)
        pulse = lax.broadcasted_iota(jnp.int32, (slots, pulses), 1)
        c, s = unit_phasor((pulse * chosen.astype(jnp.int32)) & (pulses - 1), pulses)
        c = (c * (1.0 / math.sqrt(pulses))).astype(bf16)
        s = (s * (1.0 / math.sqrt(pulses))).astype(bf16)
        table_ref[:slots, :pulses] = c
        table_ref[:slots, pulses:] = s
        table_ref[slots:, :pulses] = -s
        table_ref[slots:, pulses:] = c

        def group(i, carry):
            for j in range(loads // groups):
                load(i * (loads // groups) + j).wait()
            for pair in range(rows // 2):
                x = x_ref[pl.ds(i * rows + 2 * pair, 2)].reshape(2 * CH, 2 * pulses)
                d = lax.dot_general(
                    table_ref[...], x, (((1,), (1,)), ((), ())), preferred_element_type=f32
                )
                for part in range(2):
                    for half in range(2):
                        rows_ref[part, pl.ds(2 * pair + half, slots, stride=pitch), :] = d[
                            part * slots : (part + 1) * slots, half * CH : (half + 1) * CH
                        ]
            for part in range(2):
                o_ref[i, :, :, part * CH : (part + 1) * CH] = (
                    rows_ref[part].reshape(slots, pitch, CH)[:, :rows].astype(bf16)
                )
            save(i).start()
            return carry

        lax.fori_loop(0, groups, group, 0)
        for i in range(groups):
            save(i).wait()

    return doppler_kernel


def doppler(samples, owner_map, owners, first, count):
    range_local, channels, double_pulses = samples.shape
    slots = owners * count
    rows, pitch, loads = 16, 24, 8
    groups = range_local // rows
    return pl.pallas_call(
        make_doppler_kernel(owners, first, count),
        out_shape=pltpu.HBM((slots, range_local, 2 * channels), bf16),
        in_specs=[
            pl.BlockSpec(memory_space=pltpu.VMEM),
            pl.BlockSpec(memory_space=pl.ANY),
        ],
        out_specs=pl.BlockSpec(memory_space=pl.ANY),
        scratch_shapes=[
            pltpu.VMEM(samples.shape, bf16),
            pltpu.VMEM((2 * slots, double_pulses), bf16),
            pltpu.VMEM((2, slots * pitch, channels), f32),
            pltpu.VMEM((groups, slots, rows, 2 * channels), bf16),
            pltpu.SemaphoreType.DMA((loads,)),
            pltpu.SemaphoreType.DMA((groups,)),
        ],
        compiler_params=pltpu.CompilerParams(vmem_limit_bytes=67_043_328),
        name="doppler",
    )(owner_map.reshape(1, -1), samples)


def make_cov_kernel(first, count, listed):
    def cov_kernel(blocks_ref, hard_ref, y_ref, o_ref, buf, sem):
        per_source = y_ref.shape[2] // RB

        def copy(i, t):
            block = blocks_ref[first + i, t]
            source = block // per_source
            row = pl.multiple_of((block % per_source) * RB, RB)
            return pltpu.make_async_copy(
                y_ref.at[source, i, pl.ds(row, RB), :], buf.at[i, t], sem.at[i, t]
            )

        for i in range(count):
            for t in range(listed):
                copy(i, t).start()
        row_of = lax.broadcasted_iota(jnp.int32, (listed * RB, 1), 0)
        f = lax.broadcasted_iota(jnp.int32, (CH, CH), 0)
        g = lax.broadcasted_iota(jnp.int32, (CH, CH), 1)
        for i in range(count):
            for t in range(listed):
                copy(i, t).wait()
        used = [
            jnp.where(hard_ref[first + i] == 1, listed * RB, NTR_EASY * RB) for i in range(count)
        ]
        rows = [
            buf[i].reshape(listed * RB, 2 * CH) * (row_of < used[i]).astype(f32).astype(bf16)
            for i in range(count)
        ]
        grams = [
            lax.dot_general(y, y, (((0,), (0,)), ((), ())), preferred_element_type=f32)
            for y in rows
        ]
        for i in range(count):
            re = grams[i][:CH, :CH] + grams[i][CH:, CH:]
            im = grams[i][CH:, :CH] - grams[i][:CH, CH:]
            o_ref[i] = jnp.where(f <= g, re, im) / used[i].astype(f32)

    return cov_kernel


def covariance(owned, blocks, hard, first):
    count = owned.shape[1]
    listed = blocks.shape[1]
    smem = pl.BlockSpec(memory_space=pltpu.SMEM)
    return pl.pallas_call(
        make_cov_kernel(first, count, listed),
        out_shape=jax.ShapeDtypeStruct((count, CH, CH), f32),
        in_specs=[smem, smem, pl.BlockSpec(memory_space=pltpu.HBM)],
        out_specs=pl.BlockSpec(memory_space=pltpu.VMEM),
        scratch_shapes=[
            pltpu.VMEM((count, listed, RB, 2 * CH), bf16),
            pltpu.SemaphoreType.DMA((count, listed)),
        ],
        compiler_params=params(16),
        name="covariance",
    )(blocks, hard, owned)


def halves(z):
    high = z.astype(bf16)
    return high, (z - high.astype(f32)).astype(bf16)


def left(z):
    high, low = halves(z)
    return jnp.concatenate([high, low, high], axis=1)


def right(z):
    high, low = halves(z)

    def real_form(x):
        return jnp.concatenate([x, jnp.concatenate([-x[:, CH:], x[:, :CH]], axis=1)], axis=0)

    big = real_form(high)
    return jnp.concatenate([big, big, real_form(low)], axis=0)


def product(a, b):
    return jnp.dot(a, b, preferred_element_type=f32)


def weights_kernel(c1_ref, c3_ref, *refs):
    *c2_refs, o_ref = refs
    twos = [(ref, j) for ref in c2_refs for j in range(ref.shape[0])]
    count = o_ref.shape[0]
    bins = range(count)
    f = lax.broadcasted_iota(jnp.int32, (CH, CH), 0)
    g = lax.broadcasted_iota(jnp.int32, (CH, CH), 1)
    eye = (f == g).astype(f32)
    eye2 = jnp.concatenate([eye, jnp.zeros_like(eye)], axis=1)
    segment = lax.axis_index("segment")
    decay = [jnp.where(segment > n, decay_rate**n, 0.0) for n in range(3)]
    a, x, e = [], [], []
    for i in bins:
        ref, j = twos[i]
        packed = decay[0] * c1_ref[i] + decay[1] * ref[j] + decay[2] * c3_ref[i]
        flipped = packed.T
        re = jnp.where(f <= g, packed, flipped) + diag_load * eye
        im = jnp.where(f > g, packed, jnp.where(f < g, -flipped, 0.0))
        scale = 1.0 / jnp.sum(jnp.sum(re * eye, axis=1, keepdims=True), axis=0, keepdims=True)
        loaded = jnp.concatenate([re, im], axis=1)
        a.append(right(loaded))
        e.append(eye2 - loaded * scale)
        x.append((eye2 + e[i]) * scale)

    def both(x, e):
        return left(jnp.concatenate([x, e], axis=0))

    for turn in range(NS_STEPS // 3):
        if turn == 0:
            e = [product(left(e[i]), right(e[i])) for i in bins]
        else:
            e = [eye2 - product(left(x[i]), a[i]) for i in bins]
        for _ in range(1 if turn == 0 else 2):
            m = [product(both(x[i], e[i]), right(e[i])) for i in bins]
            x = [x[i] + m[i][:CH] for i in bins]
            e = [m[i][CH:] for i in bins]
        x = [x[i] + product(left(x[i]), right(e[i])) for i in bins]

    c, s = unit_phasor((f * (2 * g - BEAMS)) & (2 * BEAMS - 1), 2 * BEAMS)
    steer = jnp.concatenate([c, s], axis=1) * (1.0 / math.sqrt(CH))
    table = right(steer)
    vec = [product(left(x[i]), table) for i in bins]
    for i in bins:
        inner = steer * vec[i]
        gain = jnp.sum(inner[:, :BEAMS] + inner[:, BEAMS:], axis=0, keepdims=True)
        re = (vec[i][:, :BEAMS] / gain).astype(bf16)
        im = (vec[i][:, BEAMS:] / gain).astype(bf16)
        o_ref[i, :CH, :BEAMS] = re
        o_ref[i, :CH, BEAMS:] = -im
        o_ref[i, CH:, :BEAMS] = im
        o_ref[i, CH:, BEAMS:] = re


def beam_weights(c1, c3, twos):
    count = c1.shape[0]
    vmem = pl.BlockSpec(memory_space=pltpu.VMEM)
    return pl.pallas_call(
        weights_kernel,
        out_shape=jax.ShapeDtypeStruct((count, 2 * CH, 2 * BEAMS), bf16),
        in_specs=[vmem] * (2 + len(twos)),
        out_specs=vmem,
        compiler_params=params(32),
        name="weights",
    )(c1, c3, *twos)


def earlier(cov):
    count = cov.shape[0]
    if count < 4:
        c3, c1, c2 = shifted(cov, 3), shifted(cov, 1), shifted(cov, 2)
        return c1, c3, [c2]
    c1 = shifted(cov, 1)
    c3 = shifted(cov, 3)
    split = count // 2
    return c1, c3, [shifted(c1[:split], 1), shifted(c3[split:], 3)]


def compression_table(code_phase, block_len):
    length = code_phase.shape[0]
    input_pos = jnp.arange(2 * block_len, dtype=jnp.int32)[None, :]
    output_pos = jnp.arange(block_len, dtype=jnp.int32)[:, None]
    lag_index = input_pos - output_pos
    onehot = (lag_index[:, :, None] == jnp.arange(length, dtype=jnp.int32)[None, None, :]).astype(
        jnp.float32
    )
    code_table = jnp.stack([jnp.cos(code_phase), jnp.sin(code_phase)]) / math.sqrt(length)
    table = jnp.einsum("pql,kl->kpq", onehot, code_table, precision=highest)
    return table.astype(bf16).reshape(2 * block_len, 2 * block_len)


def compress_kernel(table_ref, y_hbm, z_hbm, y_ref, z_ref, in_sem, out_sem):
    count, sources, per, _ = y_ref.shape
    step = CBLK // per
    half = CH

    def load(i):
        return pltpu.make_async_copy(y_hbm.at[:, i], y_ref.at[i], in_sem.at[i])

    def save(i):
        return pltpu.make_async_copy(z_ref.at[i], z_hbm.at[i], out_sem.at[i])

    for i in range(count):
        load(i).start()
    for i in range(count):
        load(i).wait()
        for start in range(0, sources, step):
            stop = min(start + 2 * step, sources)
            y = y_ref[i, start:stop].reshape((stop - start) * per, 2 * half)
            m = jnp.dot(table_ref[:, : y.shape[0]], y, preferred_element_type=f32)
            r = pl.ds(start * per, CBLK)
            z_ref[i, r, :half] = (m[:CBLK, :half] + m[CBLK:, half:]).astype(bf16)
            z_ref[i, r, half:] = (m[:CBLK, half:] - m[CBLK:, :half]).astype(bf16)
        save(i).start()
    for i in range(count):
        save(i).wait()


def compress(owned, table):
    sources, count, per, width = owned.shape
    anywhere = pl.BlockSpec(memory_space=pl.ANY)
    place = pltpu.HBM if count > 3 else jax.ShapeDtypeStruct
    return pl.pallas_call(
        compress_kernel,
        out_shape=place((count, sources * per, width), bf16),
        in_specs=[pl.BlockSpec(memory_space=pltpu.VMEM), anywhere],
        out_specs=anywhere,
        scratch_shapes=[
            pltpu.VMEM((count, sources, per, width), bf16),
            pltpu.VMEM((count, sources * per, width), bf16),
            pltpu.SemaphoreType.DMA((count,)),
            pltpu.SemaphoreType.DMA((count,)),
        ],
        compiler_params=params(32),
        name="compress",
    )(table, owned)


def make_beams_kernel(first):
    def beams_kernel(w_ref, z_hbm, *refs):
        *_, o_hbm, z_ref, o_ref, in_sem, out_sem = refs
        count = z_ref.shape[0]

        def load(i):
            return pltpu.make_async_copy(z_hbm.at[i], z_ref.at[i], in_sem.at[i])

        def save(i):
            return pltpu.make_async_copy(o_ref.at[i], o_hbm.at[first + i], out_sem.at[i])

        for i in range(count):
            load(i).start()
        for i in range(count):
            load(i).wait()
            o_ref[i] = jnp.dot(z_ref[i], w_ref[i], preferred_element_type=f32).astype(bf16)
            save(i).start()
        for i in range(count):
            save(i).wait()

    return beams_kernel


def form_beams(z, weights, held, bins, first):
    count, rows, _ = z.shape
    width = weights.shape[2]
    anywhere = pl.BlockSpec(memory_space=pl.ANY)
    in_specs = [pl.BlockSpec(memory_space=pltpu.VMEM), anywhere]
    operands = [weights, z]
    aliases = {}
    if held is not None:
        in_specs.append(anywhere)
        operands.append(held)
        aliases = {2: 0}
    return pl.pallas_call(
        make_beams_kernel(first),
        out_shape=jax.ShapeDtypeStruct((bins, rows, width), bf16),
        in_specs=in_specs,
        out_specs=anywhere,
        scratch_shapes=[
            pltpu.VMEM(z.shape, bf16),
            pltpu.VMEM((count, rows, width), bf16),
            pltpu.SemaphoreType.DMA((count,)),
            pltpu.SemaphoreType.DMA((count,)),
        ],
        input_output_aliases=aliases,
        compiler_params=params(63 if count > 3 else 32),
        name="beams",
    )(*operands)


def chain(echoes, train_blocks, hard_bins, owner_map, code_phase):
    samples = echoes[0]
    blocks, hard = train_blocks[0], hard_bins[0]
    owners = lax.axis_size("blk")
    bins = hard.shape[0]
    firsts = [sum(CHUNKS[:i]) for i in range(len(CHUNKS))]
    spectra = []
    for first, count in zip(firsts, CHUNKS):
        sent = doppler(samples, owner_map, owners, first, count)
        spectra.append(sent.reshape(owners, count, samples.shape[0], 2 * CH))
    code_phase, spectra[0] = lax.optimization_barrier((code_phase, spectra[0]))
    table = compression_table(code_phase, CBLK)
    owned = []
    for g, sent in enumerate(spectra):
        if g > 0:
            sent, owned[-1] = lax.optimization_barrier((sent, owned[-1]))
        owned.append(lax.all_to_all(sent, "blk", split_axis=0, concat_axis=0, tiled=True))
    result = None
    for first, y in zip(firsts, owned):
        cov = covariance(y, blocks, hard, first)
        c1, c3, twos = earlier(cov)
        z = compress(y, table)
        weights = beam_weights(c1, c3, twos)
        result = form_beams(z, weights, result, bins, first)
    return result[None]


def solution(mesh):
    in_specs = (
        P("segment", "blk", None, None),
        P("segment", "blk", None),
        P("segment", "blk"),
        P(),
        P(),
    )
    out_specs = P("segment", "blk", None, None)
    return jax.shard_map(chain, mesh=mesh, in_specs=in_specs, out_specs=out_specs, check_vma=False)
```

```python
import math

import jax
import jax.numpy as jnp
from jax import lax
from jax.experimental import pallas as pl
from jax.experimental.pallas import tpu as pltpu
from jax.sharding import PartitionSpec as P


CH = 128
BEAMS = 128
RB = 32
NTR_EASY = 3
NS_STEPS = 12
CBLK = 128
CHUNKS = (5, 3)
RESIDENT = 3

decay_rate = 0.7
diag_load = 0.1
highest = lax.Precision.HIGHEST
f32 = jnp.float32
bf16 = jnp.bfloat16
MiB = 1 << 20


def params(limit=48):
    return pltpu.CompilerParams(vmem_limit_bytes=limit * MiB)


def shifted(x, by):
    peers = lax.axis_size("segment")
    return lax.ppermute(x, "segment", [(i, (i + by) % peers) for i in range(peers)])


def unit_phasor(index, period):
    eighth = period // 8
    turned = index + eighth
    quadrant = lax.shift_right_logical(turned, int(math.log2(period // 4))) & 3
    rest = (turned & (period // 4 - 1)) - eighth
    x = rest.astype(f32) * (2.0 * math.pi / period)
    x2 = x * x
    sine = x + x * x2 * (-1.0 / 6 + x2 * (1.0 / 120 + x2 * (-1.0 / 5040 + x2 * (1.0 / 362880))))
    cosine = 1.0 + x2 * (
        -0.5 + x2 * (1.0 / 24 + x2 * (-1.0 / 720 + x2 * (1.0 / 40320 - x2 * (1.0 / 3628800))))
    )
    swap = (quadrant & 1) == 1
    c = jnp.where(swap, sine, cosine)
    s = jnp.where(swap, cosine, sine)
    c = jnp.where((quadrant == 1) | (quadrant == 2), -c, c)
    s = jnp.where(quadrant >= 2, -s, s)
    return c, s


def make_doppler_kernel(owners, first, count):
    def doppler_kernel(map_ref, x_hbm, o_hbm, x_ref, table_ref, rows_ref, o_ref, in_sem, out_sem):
        slots = owners * count
        total = map_ref.shape[1]
        bins = total // owners
        pulses = x_ref.shape[2] // 2
        groups, _, rows, _ = o_ref.shape
        pitch = rows_ref.shape[1] // slots
        loads = in_sem.shape[0]
        per_load = x_ref.shape[0] // loads

        def load(i):
            piece = pl.ds(i * per_load, per_load)
            return pltpu.make_async_copy(x_hbm.at[piece], x_ref.at[piece], in_sem.at[i])

        def save(i):
            piece = o_hbm.at[:, pl.ds(i * rows, rows), :]
            return pltpu.make_async_copy(o_ref.at[i], piece, out_sem.at[i])

        for i in range(loads):
            load(i).start()
        slot = lax.broadcasted_iota(jnp.int32, (slots, total), 1)
        row = lax.broadcasted_iota(jnp.int32, (slots, total), 0)
        place = slot % bins - first
        mine = (place >= 0) & (place < count) & (slot // bins * count + place == row)
        chosen = jnp.sum(jnp.where(mine, map_ref[...].astype(f32), 0.0), axis=1, keepdims=True)
        pulse = lax.broadcasted_iota(jnp.int32, (slots, pulses), 1)
        c, s = unit_phasor((pulse * chosen.astype(jnp.int32)) & (pulses - 1), pulses)
        c = (c * (1.0 / math.sqrt(pulses))).astype(bf16)
        s = (s * (1.0 / math.sqrt(pulses))).astype(bf16)
        table_ref[:slots, :pulses] = c
        table_ref[:slots, pulses:] = s
        table_ref[slots:, :pulses] = -s
        table_ref[slots:, pulses:] = c

        def group(i, carry):
            for j in range(loads // groups):
                load(i * (loads // groups) + j).wait()
            for pair in range(rows // 2):
                x = x_ref[pl.ds(i * rows + 2 * pair, 2)].reshape(2 * CH, 2 * pulses)
                d = lax.dot_general(
                    table_ref[...], x, (((1,), (1,)), ((), ())), preferred_element_type=f32
                )
                for part in range(2):
                    for half in range(2):
                        rows_ref[part, pl.ds(2 * pair + half, slots, stride=pitch), :] = d[
                            part * slots : (part + 1) * slots, half * CH : (half + 1) * CH
                        ]
            for part in range(2):
                o_ref[i, :, :, part * CH : (part + 1) * CH] = (
                    rows_ref[part].reshape(slots, pitch, CH)[:, :rows].astype(bf16)
                )
            save(i).start()
            return carry

        lax.fori_loop(0, groups, group, 0)
        for i in range(groups):
            save(i).wait()

    return doppler_kernel


def doppler(samples, owner_map, owners, first, count):
    range_local, channels, double_pulses = samples.shape
    slots = owners * count
    rows, pitch, loads = 16, 24, 8
    groups = range_local // rows
    return pl.pallas_call(
        make_doppler_kernel(owners, first, count),
        out_shape=pltpu.HBM((slots, range_local, 2 * channels), bf16),
        in_specs=[
            pl.BlockSpec(memory_space=pltpu.VMEM),
            pl.BlockSpec(memory_space=pl.ANY),
        ],
        out_specs=pl.BlockSpec(memory_space=pl.ANY),
        scratch_shapes=[
            pltpu.VMEM(samples.shape, bf16),
            pltpu.VMEM((2 * slots, double_pulses), bf16),
            pltpu.VMEM((2, slots * pitch, channels), f32),
            pltpu.VMEM((groups, slots, rows, 2 * channels), bf16),
            pltpu.SemaphoreType.DMA((loads,)),
            pltpu.SemaphoreType.DMA((groups,)),
        ],
        compiler_params=pltpu.CompilerParams(vmem_limit_bytes=67_043_328),
        name="doppler",
    )(owner_map.reshape(1, -1), samples)


def entries(refs):
    return [(ref, j) for ref in refs for j in range(ref.shape[0])]


def make_cov_kernel(first, count, listed):
    def cov_kernel(blocks_ref, hard_ref, y_ref, *refs):
        *o_refs, buf, sem = refs
        per_source = y_ref.shape[2] // RB

        def copy(i, t):
            block = blocks_ref[first + i, t]
            source = block // per_source
            row = pl.multiple_of((block % per_source) * RB, RB)
            return pltpu.make_async_copy(
                y_ref.at[source, i, pl.ds(row, RB), :], buf.at[i, t], sem.at[i, t]
            )

        for i in range(count):
            for t in range(listed):
                copy(i, t).start()
        row_of = lax.broadcasted_iota(jnp.int32, (listed * RB, 1), 0)
        f = lax.broadcasted_iota(jnp.int32, (CH, CH), 0)
        g = lax.broadcasted_iota(jnp.int32, (CH, CH), 1)
        for i in range(count):
            for t in range(listed):
                copy(i, t).wait()
        used = [
            jnp.where(hard_ref[first + i] == 1, listed * RB, NTR_EASY * RB) for i in range(count)
        ]
        rows = [
            buf[i].reshape(listed * RB, 2 * CH) * (row_of < used[i]).astype(f32).astype(bf16)
            for i in range(count)
        ]
        grams = [
            lax.dot_general(y, y, (((0,), (0,)), ((), ())), preferred_element_type=f32)
            for y in rows
        ]
        for i, (o_ref, j) in enumerate(entries(o_refs)):
            re = grams[i][:CH, :CH] + grams[i][CH:, CH:]
            im = grams[i][CH:, :CH] - grams[i][:CH, CH:]
            o_ref[j] = jnp.where(f <= g, re, im) / used[i].astype(f32)

    return cov_kernel


def covariance(owned, blocks, hard, first, pieces):
    count = owned.shape[1]
    listed = blocks.shape[1]
    smem = pl.BlockSpec(memory_space=pltpu.SMEM)
    return pl.pallas_call(
        make_cov_kernel(first, count, listed),
        out_shape=[jax.ShapeDtypeStruct((n, CH, CH), f32) for n in pieces],
        in_specs=[smem, smem, pl.BlockSpec(memory_space=pltpu.HBM)],
        out_specs=[pl.BlockSpec(memory_space=pltpu.VMEM)] * len(pieces),
        scratch_shapes=[
            pltpu.VMEM((count, listed, RB, 2 * CH), bf16),
            pltpu.SemaphoreType.DMA((count, listed)),
        ],
        compiler_params=params(16),
        name="covariance",
    )(blocks, hard, owned)


def halves(z):
    high = z.astype(bf16)
    return high, (z - high.astype(f32)).astype(bf16)


def left(z):
    high, low = halves(z)
    return jnp.concatenate([high, low, high], axis=1)


def right(z):
    high, low = halves(z)

    def real_form(x):
        return jnp.concatenate([x, jnp.concatenate([-x[:, CH:], x[:, :CH]], axis=1)], axis=0)

    big = real_form(high)
    return jnp.concatenate([big, big, real_form(low)], axis=0)


def product(a, b):
    return jnp.dot(a, b, preferred_element_type=f32)


def weights_kernel(*refs):
    *c_refs, o_ref = refs
    parts = len(c_refs) // 3
    earlier_refs = [entries(c_refs[n * parts : (n + 1) * parts]) for n in range(3)]
    count = o_ref.shape[0]
    bins = range(count)
    f = lax.broadcasted_iota(jnp.int32, (CH, CH), 0)
    g = lax.broadcasted_iota(jnp.int32, (CH, CH), 1)
    eye = (f == g).astype(f32)
    eye2 = jnp.concatenate([eye, jnp.zeros_like(eye)], axis=1)
    segment = lax.axis_index("segment")
    decay = [jnp.where(segment > n, decay_rate**n, 0.0) for n in range(3)]
    a, x, e = [], [], []
    for i in bins:
        terms = [decay[n] * ref[j] for n in range(3) for ref, j in (earlier_refs[n][i],)]
        packed = terms[0] + terms[1] + terms[2]
        flipped = packed.T
        re = jnp.where(f <= g, packed, flipped) + diag_load * eye
        im = jnp.where(f > g, packed, jnp.where(f < g, -flipped, 0.0))
        scale = 1.0 / jnp.sum(jnp.sum(re * eye, axis=1, keepdims=True), axis=0, keepdims=True)
        loaded = jnp.concatenate([re, im], axis=1)
        a.append(right(loaded))
        e.append(eye2 - loaded * scale)
        x.append((eye2 + e[i]) * scale)

    def both(x, e):
        return left(jnp.concatenate([x, e], axis=0))

    for turn in range(NS_STEPS // 3):
        if turn == 0:
            e = [product(left(e[i]), right(e[i])) for i in bins]
        else:
            e = [eye2 - product(left(x[i]), a[i]) for i in bins]
        for _ in range(1 if turn == 0 else 2):
            m = [product(both(x[i], e[i]), right(e[i])) for i in bins]
            x = [x[i] + m[i][:CH] for i in bins]
            e = [m[i][CH:] for i in bins]
        x = [x[i] + product(left(x[i]), right(e[i])) for i in bins]

    c, s = unit_phasor((f * (2 * g - BEAMS)) & (2 * BEAMS - 1), 2 * BEAMS)
    steer = jnp.concatenate([c, s], axis=1) * (1.0 / math.sqrt(CH))
    table = right(steer)
    vec = [product(left(x[i]), table) for i in bins]
    for i in bins:
        inner = steer * vec[i]
        gain = jnp.sum(inner[:, :BEAMS] + inner[:, BEAMS:], axis=0, keepdims=True)
        re = (vec[i][:, :BEAMS] / gain).astype(bf16)
        im = (vec[i][:, BEAMS:] / gain).astype(bf16)
        o_ref[i, :CH, :BEAMS] = re
        o_ref[i, :CH, BEAMS:] = -im
        o_ref[i, CH:, :BEAMS] = im
        o_ref[i, CH:, BEAMS:] = re


def beam_weights(parts):
    count = sum(part.shape[0] for part in parts[0])
    vmem = pl.BlockSpec(memory_space=pltpu.VMEM)
    operands = [part for back in parts for part in back]
    return pl.pallas_call(
        weights_kernel,
        out_shape=jax.ShapeDtypeStruct((count, 2 * CH, 2 * BEAMS), bf16),
        in_specs=[vmem] * len(operands),
        out_specs=vmem,
        compiler_params=params(32),
        name="weights",
    )(*operands)


def earlier(cov):
    if len(cov) == 1:
        c3, c1, c2 = (shifted(cov[0], by) for by in (3, 1, 2))
        return [c1], [c2], [c3]
    low, high = cov
    low1, high3 = shifted(low, 1), shifted(high, 3)
    high1, low3 = shifted(high, 1), shifted(low, 3)
    low2, high2 = shifted(low1, 1), shifted(high3, 3)
    return [low1, high1], [low2, high2], [low3, high3]


def compression_table(code_phase, block_len):
    length = code_phase.shape[0]
    input_pos = jnp.arange(2 * block_len, dtype=jnp.int32)[None, :]
    output_pos = jnp.arange(block_len, dtype=jnp.int32)[:, None]
    lag_index = input_pos - output_pos
    onehot = (lag_index[:, :, None] == jnp.arange(length, dtype=jnp.int32)[None, None, :]).astype(
        jnp.float32
    )
    code_table = jnp.stack([jnp.cos(code_phase), jnp.sin(code_phase)]) / math.sqrt(length)
    table = jnp.einsum("pql,kl->kpq", onehot, code_table, precision=highest)
    return table.astype(bf16).reshape(2 * block_len, 2 * block_len)


def compress_kernel(table_ref, y_hbm, z_out, y_ref, in_sem, *held):
    count, sources, per, _ = y_ref.shape
    z_ref, out_sem = held if held else (z_out, None)
    step = CBLK // per
    half = CH

    def load(i):
        return pltpu.make_async_copy(y_hbm.at[:, i], y_ref.at[i], in_sem.at[i])

    def save(i):
        return pltpu.make_async_copy(z_ref.at[i], z_out.at[i], out_sem.at[i])

    for i in range(count):
        load(i).start()
    for i in range(count):
        load(i).wait()
        for start in range(0, sources, step):
            stop = min(start + 2 * step, sources)
            y = y_ref[i, start:stop].reshape((stop - start) * per, 2 * half)
            m = jnp.dot(table_ref[:, : y.shape[0]], y, preferred_element_type=f32)
            r = pl.ds(start * per, CBLK)
            z_ref[i, r, :half] = (m[:CBLK, :half] + m[CBLK:, half:]).astype(bf16)
            z_ref[i, r, half:] = (m[:CBLK, half:] - m[CBLK:, :half]).astype(bf16)
        if held:
            save(i).start()
    if held:
        for i in range(count):
            save(i).wait()


def compress(owned, table):
    sources, count, per, width = owned.shape
    vmem = pl.BlockSpec(memory_space=pltpu.VMEM)
    anywhere = pl.BlockSpec(memory_space=pl.ANY)
    shape = (count, sources * per, width)
    scratch = [
        pltpu.VMEM((count, sources, per, width), bf16),
        pltpu.SemaphoreType.DMA((count,)),
    ]
    if count > RESIDENT:
        scratch += [pltpu.VMEM(shape, bf16), pltpu.SemaphoreType.DMA((count,))]
    return pl.pallas_call(
        compress_kernel,
        out_shape=pltpu.HBM(shape, bf16) if count > RESIDENT else jax.ShapeDtypeStruct(shape, bf16),
        in_specs=[vmem, anywhere],
        out_specs=anywhere if count > RESIDENT else vmem,
        scratch_shapes=scratch,
        compiler_params=params(32),
        name="compress",
    )(table, owned)


def make_beams_kernel(first, aliased):
    def beams_kernel(w_ref, z_in, *refs):
        o_hbm, o_ref, out_sem, *held = refs[aliased:]
        z_ref, in_sem = held if held else (z_in, None)
        count, rows, _ = z_ref.shape
        pieces = out_sem.shape[1]
        step = rows // pieces

        def load(i):
            return pltpu.make_async_copy(z_in.at[i], z_ref.at[i], in_sem.at[i])

        def save(i, p):
            piece = pl.ds(p * step, step)
            return pltpu.make_async_copy(
                o_ref.at[i, piece], o_hbm.at[first + i, piece], out_sem.at[i, p]
            )

        if held:
            for i in range(count):
                load(i).start()
        for i in range(count):
            if held:
                load(i).wait()
            for p in range(pieces):
                r = pl.ds(p * step, step)
                o_ref[i, r] = jnp.dot(
                    z_ref[i, r], w_ref[i], preferred_element_type=f32
                ).astype(bf16)
                save(i, p).start()
        for i in range(count):
            for p in range(pieces):
                save(i, p).wait()

    return beams_kernel


def form_beams(z, weights, held, bins, first):
    count, rows, _ = z.shape
    width = weights.shape[2]
    resident = count <= RESIDENT
    vmem = pl.BlockSpec(memory_space=pltpu.VMEM)
    anywhere = pl.BlockSpec(memory_space=pl.ANY)
    in_specs = [vmem, vmem if resident else anywhere]
    operands = [weights, z]
    aliases = {}
    if held is not None:
        in_specs.append(anywhere)
        operands.append(held)
        aliases = {2: 0}
    pieces = 2 if resident else 1
    scratch = [
        pltpu.VMEM((count, rows, width), bf16),
        pltpu.SemaphoreType.DMA((count, pieces)),
    ]
    if not resident:
        scratch += [pltpu.VMEM(z.shape, bf16), pltpu.SemaphoreType.DMA((count,))]
    return pl.pallas_call(
        make_beams_kernel(first, len(aliases)),
        out_shape=jax.ShapeDtypeStruct((bins, rows, width), bf16),
        in_specs=in_specs,
        out_specs=anywhere,
        scratch_shapes=scratch,
        input_output_aliases=aliases,
        compiler_params=params(32 if resident else 59),
        name="beams",
    )(*operands)


def chain(echoes, train_blocks, hard_bins, owner_map, code_phase):
    samples = echoes[0]
    blocks, hard = train_blocks[0], hard_bins[0]
    owners = lax.axis_size("blk")
    bins = hard.shape[0]
    firsts = [sum(CHUNKS[:i]) for i in range(len(CHUNKS))]
    spectra = []
    for first, count in zip(firsts, CHUNKS):
        sent = doppler(samples, owner_map, owners, first, count)
        spectra.append(sent.reshape(owners, count, samples.shape[0], 2 * CH))
    code_phase, spectra[0] = lax.optimization_barrier((code_phase, spectra[0]))
    table = compression_table(code_phase, CBLK)
    owned = []
    for g, sent in enumerate(spectra):
        if g > 0:
            sent, owned[-1] = lax.optimization_barrier((sent, owned[-1]))
        owned.append(lax.all_to_all(sent, "blk", split_axis=0, concat_axis=0, tiled=True))
    result = None
    for first, y in zip(firsts, owned):
        count = y.shape[1]
        pieces = [count // 2, count - count // 2] if count > 2 else [count]
        parts = earlier(covariance(y, blocks, hard, first, pieces))
        z = compress(y, table)
        weights = beam_weights(parts)
        result = form_beams(z, weights, result, bins, first)
    return result[None]


def solution(mesh):
    in_specs = (
        P("segment", "blk", None, None),
        P("segment", "blk", None),
        P("segment", "blk"),
        P(),
        P(),
    )
    out_specs = P("segment", "blk", None, None)
    return jax.shard_map(chain, mesh=mesh, in_specs=in_specs, out_specs=out_specs, check_vma=False)
```

```python
import math

import jax
import jax.numpy as jnp
from jax import lax
from jax.experimental import pallas as pl
from jax.experimental.pallas import tpu as pltpu
from jax.sharding import PartitionSpec as P


CH = 128
BEAMS = 128
RB = 32
NTR_EASY = 3
NS_STEPS = 12
CBLK = 128
CHUNKS = (6, 2)
EARLY = 2

decay_rate = 0.7
diag_load = 0.1
highest = lax.Precision.HIGHEST
f32 = jnp.float32
bf16 = jnp.bfloat16
MiB = 1 << 20


def params(limit=48):
    return pltpu.CompilerParams(vmem_limit_bytes=limit * MiB)


def shifted(x, by):
    peers = lax.axis_size("segment")
    return lax.ppermute(x, "segment", [(i, (i + by) % peers) for i in range(peers)])


def unit_phasor(index, period):
    eighth = period // 8
    turned = index + eighth
    quadrant = lax.shift_right_logical(turned, int(math.log2(period // 4))) & 3
    rest = (turned & (period // 4 - 1)) - eighth
    x = rest.astype(f32) * (2.0 * math.pi / period)
    x2 = x * x
    sine = x + x * x2 * (-1.0 / 6 + x2 * (1.0 / 120 + x2 * (-1.0 / 5040 + x2 * (1.0 / 362880))))
    cosine = 1.0 + x2 * (
        -0.5 + x2 * (1.0 / 24 + x2 * (-1.0 / 720 + x2 * (1.0 / 40320 - x2 * (1.0 / 3628800))))
    )
    swap = (quadrant & 1) == 1
    c = jnp.where(swap, sine, cosine)
    s = jnp.where(swap, cosine, sine)
    c = jnp.where((quadrant == 1) | (quadrant == 2), -c, c)
    s = jnp.where(quadrant >= 2, -s, s)
    return c, s


def make_doppler_kernel(owners, first, count):
    def doppler_kernel(map_ref, x_hbm, o_hbm, x_ref, table_ref, rows_ref, o_ref, in_sem, out_sem):
        slots = owners * count
        total = map_ref.shape[1]
        bins = total // owners
        pulses = x_ref.shape[2] // 2
        groups, _, rows, _ = o_ref.shape
        pitch = rows_ref.shape[1] // slots
        loads = in_sem.shape[0]
        per_load = x_ref.shape[0] // loads

        def load(i):
            piece = pl.ds(i * per_load, per_load)
            return pltpu.make_async_copy(x_hbm.at[piece], x_ref.at[piece], in_sem.at[i])

        def save(i):
            piece = o_hbm.at[:, pl.ds(i * rows, rows), :]
            return pltpu.make_async_copy(o_ref.at[i], piece, out_sem.at[i])

        for i in range(loads):
            load(i).start()
        slot = lax.broadcasted_iota(jnp.int32, (slots, total), 1)
        row = lax.broadcasted_iota(jnp.int32, (slots, total), 0)
        place = slot % bins - first
        mine = (place >= 0) & (place < count) & (slot // bins * count + place == row)
        chosen = jnp.sum(jnp.where(mine, map_ref[...].astype(f32), 0.0), axis=1, keepdims=True)
        pulse = lax.broadcasted_iota(jnp.int32, (slots, pulses), 1)
        c, s = unit_phasor((pulse * chosen.astype(jnp.int32)) & (pulses - 1), pulses)
        c = (c * (1.0 / math.sqrt(pulses))).astype(bf16)
        s = (s * (1.0 / math.sqrt(pulses))).astype(bf16)
        table_ref[:slots, :pulses] = c
        table_ref[:slots, pulses:] = s
        table_ref[slots:, :pulses] = -s
        table_ref[slots:, pulses:] = c

        def group(i, carry):
            for j in range(loads // groups):
                load(i * (loads // groups) + j).wait()
            for pair in range(rows // 2):
                x = x_ref[pl.ds(i * rows + 2 * pair, 2)].reshape(2 * CH, 2 * pulses)
                d = lax.dot_general(
                    table_ref[...], x, (((1,), (1,)), ((), ())), preferred_element_type=f32
                )
                for part in range(2):
                    for half in range(2):
                        rows_ref[part, pl.ds(2 * pair + half, slots, stride=pitch), :] = d[
                            part * slots : (part + 1) * slots, half * CH : (half + 1) * CH
                        ]
            for part in range(2):
                o_ref[i, :, :, part * CH : (part + 1) * CH] = (
                    rows_ref[part].reshape(slots, pitch, CH)[:, :rows].astype(bf16)
                )
            save(i).start()
            return carry

        lax.fori_loop(0, groups, group, 0)
        for i in range(groups):
            save(i).wait()

    return doppler_kernel


def doppler(samples, owner_map, owners, first, count):
    range_local, channels, double_pulses = samples.shape
    slots = owners * count
    rows, pitch, loads = 16, 24, 8
    groups = range_local // rows
    return pl.pallas_call(
        make_doppler_kernel(owners, first, count),
        out_shape=pltpu.HBM((slots, range_local, 2 * channels), bf16),
        in_specs=[
            pl.BlockSpec(memory_space=pltpu.VMEM),
            pl.BlockSpec(memory_space=pl.ANY),
        ],
        out_specs=pl.BlockSpec(memory_space=pl.ANY),
        scratch_shapes=[
            pltpu.VMEM(samples.shape, bf16),
            pltpu.VMEM((2 * slots, double_pulses), bf16),
            pltpu.VMEM((2, slots * pitch, channels), f32),
            pltpu.VMEM((groups, slots, rows, 2 * channels), bf16),
            pltpu.SemaphoreType.DMA((loads,)),
            pltpu.SemaphoreType.DMA((groups,)),
        ],
        compiler_params=pltpu.CompilerParams(vmem_limit_bytes=67_043_328),
        name="doppler",
    )(owner_map.reshape(1, -1), samples)


def entries(refs):
    return [(ref, j) for ref in refs for j in range(ref.shape[0])]


def make_cov_kernel(first, count, listed):
    def cov_kernel(blocks_ref, hard_ref, y_ref, *refs):
        *o_refs, buf, sem = refs
        per_source = y_ref.shape[2] // RB

        def copy(i, t):
            block = blocks_ref[first + i, t]
            source = block // per_source
            row = pl.multiple_of((block % per_source) * RB, RB)
            return pltpu.make_async_copy(
                y_ref.at[source, i, pl.ds(row, RB), :], buf.at[i, t], sem.at[i, t]
            )

        for i in range(count):
            for t in range(listed):
                copy(i, t).start()
        row_of = lax.broadcasted_iota(jnp.int32, (listed * RB, 1), 0)
        f = lax.broadcasted_iota(jnp.int32, (CH, CH), 0)
        g = lax.broadcasted_iota(jnp.int32, (CH, CH), 1)
        for i in range(count):
            for t in range(listed):
                copy(i, t).wait()
        used = [
            jnp.where(hard_ref[first + i] == 1, listed * RB, NTR_EASY * RB) for i in range(count)
        ]
        rows = [
            buf[i].reshape(listed * RB, 2 * CH) * (row_of < used[i]).astype(f32).astype(bf16)
            for i in range(count)
        ]
        grams = [
            lax.dot_general(y, y, (((0,), (0,)), ((), ())), preferred_element_type=f32)
            for y in rows
        ]
        for i, (o_ref, j) in enumerate(entries(o_refs)):
            re = grams[i][:CH, :CH] + grams[i][CH:, CH:]
            im = grams[i][CH:, :CH] - grams[i][:CH, CH:]
            o_ref[j] = jnp.where(f <= g, re, im) / used[i].astype(f32)

    return cov_kernel


def covariance(owned, blocks, hard, first, pieces):
    count = owned.shape[1]
    listed = blocks.shape[1]
    smem = pl.BlockSpec(memory_space=pltpu.SMEM)
    return pl.pallas_call(
        make_cov_kernel(first, count, listed),
        out_shape=[jax.ShapeDtypeStruct((n, CH, CH), f32) for n in pieces],
        in_specs=[smem, smem, pl.BlockSpec(memory_space=pltpu.HBM)],
        out_specs=[pl.BlockSpec(memory_space=pltpu.VMEM)] * len(pieces),
        scratch_shapes=[
            pltpu.VMEM((count, listed, RB, 2 * CH), bf16),
            pltpu.SemaphoreType.DMA((count, listed)),
        ],
        compiler_params=params(16),
        name="covariance",
    )(blocks, hard, owned)


def halves(z):
    high = z.astype(bf16)
    return high, (z - high.astype(f32)).astype(bf16)


def left(z):
    high, low = halves(z)
    return jnp.concatenate([high, low, high], axis=1)


def right(z):
    high, low = halves(z)

    def real_form(x):
        return jnp.concatenate([x, jnp.concatenate([-x[:, CH:], x[:, :CH]], axis=1)], axis=0)

    big = real_form(high)
    return jnp.concatenate([big, big, real_form(low)], axis=0)


def product(a, b):
    return jnp.dot(a, b, preferred_element_type=f32)


def weights_kernel(*refs):
    *c_refs, o_ref = refs
    parts = len(c_refs) // 3
    earlier_refs = [entries(c_refs[n * parts : (n + 1) * parts]) for n in range(3)]
    count = o_ref.shape[0]
    bins = range(count)
    f = lax.broadcasted_iota(jnp.int32, (CH, CH), 0)
    g = lax.broadcasted_iota(jnp.int32, (CH, CH), 1)
    eye = (f == g).astype(f32)
    eye2 = jnp.concatenate([eye, jnp.zeros_like(eye)], axis=1)
    segment = lax.axis_index("segment")
    decay = [jnp.where(segment > n, decay_rate**n, 0.0) for n in range(3)]
    a, x, e = [], [], []
    for i in bins:
        terms = [decay[n] * ref[j] for n in range(3) for ref, j in (earlier_refs[n][i],)]
        packed = terms[0] + terms[1] + terms[2]
        flipped = packed.T
        re = jnp.where(f <= g, packed, flipped) + diag_load * eye
        im = jnp.where(f > g, packed, jnp.where(f < g, -flipped, 0.0))
        scale = 1.0 / jnp.sum(jnp.sum(re * eye, axis=1, keepdims=True), axis=0, keepdims=True)
        loaded = jnp.concatenate([re, im], axis=1)
        a.append(right(loaded))
        e.append(eye2 - loaded * scale)
        x.append((eye2 + e[i]) * scale)

    def both(x, e):
        return left(jnp.concatenate([x, e], axis=0))

    for turn in range(NS_STEPS // 3):
        if turn == 0:
            e = [product(left(e[i]), right(e[i])) for i in bins]
        else:
            e = [eye2 - product(left(x[i]), a[i]) for i in bins]
        for _ in range(1 if turn == 0 else 2):
            m = [product(both(x[i], e[i]), right(e[i])) for i in bins]
            x = [x[i] + m[i][:CH] for i in bins]
            e = [m[i][CH:] for i in bins]
        x = [x[i] + product(left(x[i]), right(e[i])) for i in bins]

    c, s = unit_phasor((f * (2 * g - BEAMS)) & (2 * BEAMS - 1), 2 * BEAMS)
    steer = jnp.concatenate([c, s], axis=1) * (1.0 / math.sqrt(CH))
    table = right(steer)
    vec = [product(left(x[i]), table) for i in bins]
    for i in bins:
        inner = steer * vec[i]
        gain = jnp.sum(inner[:, :BEAMS] + inner[:, BEAMS:], axis=0, keepdims=True)
        re = (vec[i][:, :BEAMS] / gain).astype(bf16)
        im = (vec[i][:, BEAMS:] / gain).astype(bf16)
        o_ref[i, :CH, :BEAMS] = re
        o_ref[i, :CH, BEAMS:] = -im
        o_ref[i, CH:, :BEAMS] = im
        o_ref[i, CH:, BEAMS:] = re


def beam_weights(parts):
    count = sum(part.shape[0] for part in parts[0])
    vmem = pl.BlockSpec(memory_space=pltpu.VMEM)
    operands = [part for back in parts for part in back]
    return pl.pallas_call(
        weights_kernel,
        out_shape=jax.ShapeDtypeStruct((count, 2 * CH, 2 * BEAMS), bf16),
        in_specs=[vmem] * len(operands),
        out_specs=vmem,
        compiler_params=params(32),
        name="weights",
    )(*operands)


def earlier(cov):
    if len(cov) == 1:
        c3, c1, c2 = (shifted(cov[0], by) for by in (3, 1, 2))
        return [c1], [c2], [c3]
    low, high = cov
    low1, high3 = shifted(low, 1), shifted(high, 3)
    high1, low3 = shifted(high, 1), shifted(low, 3)
    low2, high2 = shifted(low1, 1), shifted(high3, 3)
    return [low1, high1], [low2, high2], [low3, high3]


def compression_table(code_phase, block_len):
    length = code_phase.shape[0]
    input_pos = jnp.arange(2 * block_len, dtype=jnp.int32)[None, :]
    output_pos = jnp.arange(block_len, dtype=jnp.int32)[:, None]
    lag_index = input_pos - output_pos
    onehot = (lag_index[:, :, None] == jnp.arange(length, dtype=jnp.int32)[None, None, :]).astype(
        jnp.float32
    )
    code_table = jnp.stack([jnp.cos(code_phase), jnp.sin(code_phase)]) / math.sqrt(length)
    table = jnp.einsum("pql,kl->kpq", onehot, code_table, precision=highest)
    return table.astype(bf16).reshape(2 * block_len, 2 * block_len)


def compress_rows(table_ref, y_ref, z_ref):
    sources, per, _ = y_ref.shape
    step = CBLK // per
    half = CH
    for start in range(0, sources, step):
        stop = min(start + 2 * step, sources)
        y = y_ref[start:stop].reshape((stop - start) * per, 2 * half)
        m = jnp.dot(table_ref[:, : y.shape[0]], y, preferred_element_type=f32)
        r = pl.ds(start * per, CBLK)
        z_ref[r, :half] = (m[:CBLK, :half] + m[CBLK:, half:]).astype(bf16)
        z_ref[r, half:] = (m[:CBLK, half:] - m[CBLK:, :half]).astype(bf16)


def compress_kernel(table_ref, y_hbm, z_ref, y_ref, sem):
    def load(i):
        return pltpu.make_async_copy(y_hbm.at[:, i], y_ref.at[i], sem.at[i])

    count = y_ref.shape[0]
    for i in range(count):
        load(i).start()
    for i in range(count):
        load(i).wait()
        compress_rows(table_ref, y_ref.at[i], z_ref.at[i])


def compress(owned, table):
    sources, count, per, width = owned.shape
    vmem = pl.BlockSpec(memory_space=pltpu.VMEM)
    return pl.pallas_call(
        compress_kernel,
        out_shape=jax.ShapeDtypeStruct((count, sources * per, width), bf16),
        in_specs=[vmem, pl.BlockSpec(memory_space=pl.ANY)],
        out_specs=vmem,
        scratch_shapes=[
            pltpu.VMEM((count, sources, per, width), bf16),
            pltpu.SemaphoreType.DMA((count,)),
        ],
        compiler_params=params(32),
        name="compress",
    )(table, owned)


def make_beams_kernel(first, aliased):
    def beams_kernel(w_ref, z_ref, *refs):
        o_hbm, o_ref, sem = refs[aliased:]
        count, rows, _ = z_ref.shape
        pieces = sem.shape[1]
        step = rows // pieces

        def save(i, p):
            r = pl.ds(p * step, step)
            return pltpu.make_async_copy(o_ref.at[i, r], o_hbm.at[first + i, r], sem.at[i, p])

        for i in range(count):
            for p in range(pieces):
                r = pl.ds(p * step, step)
                o_ref[i, r] = jnp.dot(z_ref[i, r], w_ref[i], preferred_element_type=f32).astype(
                    bf16
                )
                save(i, p).start()
        for i in range(count):
            for p in range(pieces):
                save(i, p).wait()

    return beams_kernel


def form_beams(z, weights, held, bins, first):
    count, rows, _ = z.shape
    width = weights.shape[2]
    vmem = pl.BlockSpec(memory_space=pltpu.VMEM)
    anywhere = pl.BlockSpec(memory_space=pl.ANY)
    before = [] if held is None else [held]
    return pl.pallas_call(
        make_beams_kernel(first, len(before)),
        out_shape=jax.ShapeDtypeStruct((bins, rows, width), bf16),
        in_specs=[vmem, vmem] + [anywhere] * len(before),
        out_specs=anywhere,
        scratch_shapes=[
            pltpu.VMEM((count, rows, width), bf16),
            pltpu.SemaphoreType.DMA((count, 2)),
        ],
        input_output_aliases={2: 0} if before else {},
        compiler_params=params(32),
        name="beams",
    )(weights, z, *before)


def make_returns_kernel(first, skip, aliased):
    def returns_kernel(table_ref, w_ref, y_hbm, *refs):
        o_hbm, y_ref, z_ref, o_ref, in_sem, out_sem = refs[aliased:]
        count = y_ref.shape[0]

        def load(i):
            return pltpu.make_async_copy(y_hbm.at[:, skip + i], y_ref.at[i], in_sem.at[i])

        def save(i):
            return pltpu.make_async_copy(o_ref.at[i], o_hbm.at[first + skip + i], out_sem.at[i])

        for i in range(count):
            load(i).start()
        for i in range(count):
            load(i).wait()
            compress_rows(table_ref, y_ref.at[i], z_ref.at[i])
            o_ref[i] = jnp.dot(z_ref[i], w_ref[skip + i], preferred_element_type=f32).astype(bf16)
            save(i).start()
        for i in range(count):
            save(i).wait()

    return returns_kernel


def form_returns(owned, table, weights, held, bins, first, skip, count):
    sources, _, per, _ = owned.shape
    width = weights.shape[2]
    rows = sources * per
    vmem = pl.BlockSpec(memory_space=pltpu.VMEM)
    anywhere = pl.BlockSpec(memory_space=pl.ANY)
    before = [] if held is None else [held]
    return pl.pallas_call(
        make_returns_kernel(first, skip, len(before)),
        out_shape=jax.ShapeDtypeStruct((bins, rows, width), bf16),
        in_specs=[vmem, vmem, anywhere] + [anywhere] * len(before),
        out_specs=anywhere,
        scratch_shapes=[
            pltpu.VMEM((count, sources, per, owned.shape[3]), bf16),
            pltpu.VMEM((count, rows, owned.shape[3]), bf16),
            pltpu.VMEM((count, rows, width), bf16),
            pltpu.SemaphoreType.DMA((count,)),
            pltpu.SemaphoreType.DMA((count,)),
        ],
        input_output_aliases={3: 0} if before else {},
        compiler_params=params(59),
        name="returns",
    )(table, weights, owned, *before)


def chain(echoes, train_blocks, hard_bins, owner_map, code_phase):
    samples = echoes[0]
    blocks, hard = train_blocks[0], hard_bins[0]
    owners = lax.axis_size("blk")
    bins = hard.shape[0]
    firsts = [sum(CHUNKS[:i]) for i in range(len(CHUNKS))]
    spectra = []
    for first, count in zip(firsts, CHUNKS):
        sent = doppler(samples, owner_map, owners, first, count)
        spectra.append(sent.reshape(owners, count, samples.shape[0], 2 * CH))
    code_phase, spectra[0] = lax.optimization_barrier((code_phase, spectra[0]))
    table = compression_table(code_phase, CBLK)
    owned = []
    for g, sent in enumerate(spectra):
        if g > 0:
            sent, owned[-1] = lax.optimization_barrier((sent, owned[-1]))
        owned.append(lax.all_to_all(sent, "blk", split_axis=0, concat_axis=0, tiled=True))
    result = None
    for g, (first, y) in enumerate(zip(firsts, owned)):
        count = y.shape[1]
        pieces = [count // 2, count - count // 2] if count > 2 else [count]
        parts = earlier(covariance(y, blocks, hard, first, pieces))
        if g == len(CHUNKS) - 1:
            z = compress(y, table)
            result = form_beams(z, beam_weights(parts), result, bins, first)
            continue
        weights = beam_weights(parts)
        for skip, some in ((0, EARLY), (EARLY, count - EARLY)):
            result = form_returns(y, table, weights, result, bins, first, skip, some)
    return result[None]


def solution(mesh):
    in_specs = (
        P("segment", "blk", None, None),
        P("segment", "blk", None),
        P("segment", "blk"),
        P(),
        P(),
    )
    out_specs = P("segment", "blk", None, None)
    return jax.shard_map(chain, mesh=mesh, in_specs=in_specs, out_specs=out_specs, check_vma=False)
```

```python
import math

import jax
import jax.numpy as jnp
from jax import lax
from jax.experimental import pallas as pl
from jax.experimental.pallas import tpu as pltpu
from jax.sharding import PartitionSpec as P


CH = 128
BEAMS = 128
RB = 32
NTR_EASY = 3
NS_STEPS = 12
CBLK = 128
CHUNKS = (6, 2)
EARLY = 2

decay_rate = 0.7
diag_load = 0.1
highest = lax.Precision.HIGHEST
f32 = jnp.float32
bf16 = jnp.bfloat16
MiB = 1 << 20


def params(limit=48):
    return pltpu.CompilerParams(vmem_limit_bytes=limit * MiB)


def shifted(x, by):
    peers = lax.axis_size("segment")
    return lax.ppermute(x, "segment", [(i, (i + by) % peers) for i in range(peers)])


def unit_phasor(index, period):
    eighth = period // 8
    turned = index + eighth
    quadrant = lax.shift_right_logical(turned, int(math.log2(period // 4))) & 3
    rest = (turned & (period // 4 - 1)) - eighth
    x = rest.astype(f32) * (2.0 * math.pi / period)
    x2 = x * x
    sine = x + x * x2 * (-1.0 / 6 + x2 * (1.0 / 120 + x2 * (-1.0 / 5040 + x2 * (1.0 / 362880))))
    cosine = 1.0 + x2 * (
        -0.5 + x2 * (1.0 / 24 + x2 * (-1.0 / 720 + x2 * (1.0 / 40320 - x2 * (1.0 / 3628800))))
    )
    swap = (quadrant & 1) == 1
    c = jnp.where(swap, sine, cosine)
    s = jnp.where(swap, cosine, sine)
    c = jnp.where((quadrant == 1) | (quadrant == 2), -c, c)
    s = jnp.where(quadrant >= 2, -s, s)
    return c, s


def make_doppler_kernel(owners, first, count):
    def doppler_kernel(map_ref, x_hbm, o_hbm, x_ref, table_ref, rows_ref, o_ref, in_sem, out_sem):
        slots = owners * count
        total = map_ref.shape[1]
        bins = total // owners
        pulses = x_ref.shape[2] // 2
        groups, _, rows, _ = o_ref.shape
        pitch = rows_ref.shape[1] // slots
        loads = in_sem.shape[0]
        per_load = x_ref.shape[0] // loads

        def load(i):
            piece = pl.ds(i * per_load, per_load)
            return pltpu.make_async_copy(x_hbm.at[piece], x_ref.at[piece], in_sem.at[i])

        def save(i):
            piece = o_hbm.at[:, pl.ds(i * rows, rows), :]
            return pltpu.make_async_copy(o_ref.at[i], piece, out_sem.at[i])

        for i in range(loads):
            load(i).start()
        slot = lax.broadcasted_iota(jnp.int32, (slots, total), 1)
        row = lax.broadcasted_iota(jnp.int32, (slots, total), 0)
        place = slot % bins - first
        mine = (place >= 0) & (place < count) & (slot // bins * count + place == row)
        chosen = jnp.sum(jnp.where(mine, map_ref[...].astype(f32), 0.0), axis=1, keepdims=True)
        pulse = lax.broadcasted_iota(jnp.int32, (slots, pulses), 1)
        c, s = unit_phasor((pulse * chosen.astype(jnp.int32)) & (pulses - 1), pulses)
        c = (c * (1.0 / math.sqrt(pulses))).astype(bf16)
        s = (s * (1.0 / math.sqrt(pulses))).astype(bf16)
        table_ref[:slots, :pulses] = c
        table_ref[:slots, pulses:] = s
        table_ref[slots:, :pulses] = -s
        table_ref[slots:, pulses:] = c

        def group(i, carry):
            for j in range(loads // groups):
                load(i * (loads // groups) + j).wait()
            for pair in range(rows // 2):
                x = x_ref[pl.ds(i * rows + 2 * pair, 2)].reshape(2 * CH, 2 * pulses)
                d = lax.dot_general(
                    table_ref[...], x, (((1,), (1,)), ((), ())), preferred_element_type=f32
                )
                for part in range(2):
                    for half in range(2):
                        rows_ref[part, pl.ds(2 * pair + half, slots, stride=pitch), :] = d[
                            part * slots : (part + 1) * slots, half * CH : (half + 1) * CH
                        ]
            for part in range(2):
                o_ref[i, :, :, part * CH : (part + 1) * CH] = (
                    rows_ref[part].reshape(slots, pitch, CH)[:, :rows].astype(bf16)
                )
            save(i).start()
            return carry

        lax.fori_loop(0, groups, group, 0)
        for i in range(groups):
            save(i).wait()

    return doppler_kernel


def doppler(samples, owner_map, owners, first, count):
    range_local, channels, double_pulses = samples.shape
    slots = owners * count
    rows, pitch, loads = 16, 24, 8
    groups = range_local // rows
    return pl.pallas_call(
        make_doppler_kernel(owners, first, count),
        out_shape=pltpu.HBM((slots, range_local, 2 * channels), bf16),
        in_specs=[
            pl.BlockSpec(memory_space=pltpu.VMEM),
            pl.BlockSpec(memory_space=pl.ANY),
        ],
        out_specs=pl.BlockSpec(memory_space=pl.ANY),
        scratch_shapes=[
            pltpu.VMEM(samples.shape, bf16),
            pltpu.VMEM((2 * slots, double_pulses), bf16),
            pltpu.VMEM((2, slots * pitch, channels), f32),
            pltpu.VMEM((groups, slots, rows, 2 * channels), bf16),
            pltpu.SemaphoreType.DMA((loads,)),
            pltpu.SemaphoreType.DMA((groups,)),
        ],
        compiler_params=pltpu.CompilerParams(vmem_limit_bytes=67_043_328),
        name="doppler",
    )(owner_map.reshape(1, -1), samples)


def entries(refs):
    return [(ref, j) for ref in refs for j in range(ref.shape[0])]


def make_cov_kernel(first, count, listed):
    def cov_kernel(blocks_ref, hard_ref, y_ref, *refs):
        *o_refs, buf, sem = refs
        per_source = y_ref.shape[2] // RB

        def copy(i, t):
            block = blocks_ref[first + i, t]
            source = block // per_source
            row = pl.multiple_of((block % per_source) * RB, RB)
            return pltpu.make_async_copy(
                y_ref.at[source, i, pl.ds(row, RB), :], buf.at[i, t], sem.at[i, t]
            )

        for i in range(count):
            for t in range(listed):
                copy(i, t).start()
        row_of = lax.broadcasted_iota(jnp.int32, (listed * RB, 1), 0)
        f = lax.broadcasted_iota(jnp.int32, (CH, CH), 0)
        g = lax.broadcasted_iota(jnp.int32, (CH, CH), 1)
        for i in range(count):
            for t in range(listed):
                copy(i, t).wait()
        used = [
            jnp.where(hard_ref[first + i] == 1, listed * RB, NTR_EASY * RB) for i in range(count)
        ]
        rows = [
            buf[i].reshape(listed * RB, 2 * CH) * (row_of < used[i]).astype(f32).astype(bf16)
            for i in range(count)
        ]
        grams = [
            lax.dot_general(y, y, (((0,), (0,)), ((), ())), preferred_element_type=f32)
            for y in rows
        ]
        for i, (o_ref, j) in enumerate(entries(o_refs)):
            re = grams[i][:CH, :CH] + grams[i][CH:, CH:]
            im = grams[i][CH:, :CH] - grams[i][:CH, CH:]
            o_ref[j] = jnp.where(f <= g, re, im) / used[i].astype(f32)

    return cov_kernel


def covariance(owned, blocks, hard, first, pieces):
    count = owned.shape[1]
    listed = blocks.shape[1]
    smem = pl.BlockSpec(memory_space=pltpu.SMEM)
    return pl.pallas_call(
        make_cov_kernel(first, count, listed),
        out_shape=[jax.ShapeDtypeStruct((n, CH, CH), f32) for n in pieces],
        in_specs=[smem, smem, pl.BlockSpec(memory_space=pltpu.HBM)],
        out_specs=[pl.BlockSpec(memory_space=pltpu.VMEM)] * len(pieces),
        scratch_shapes=[
            pltpu.VMEM((count, listed, RB, 2 * CH), bf16),
            pltpu.SemaphoreType.DMA((count, listed)),
        ],
        compiler_params=params(16),
        name="covariance",
    )(blocks, hard, owned)


def halves(z):
    high = z.astype(bf16)
    return high, (z - high.astype(f32)).astype(bf16)


def left(z):
    high, low = halves(z)
    return jnp.concatenate([high, low, high], axis=1)


def right(z):
    high, low = halves(z)

    def real_form(x):
        return jnp.concatenate([x, jnp.concatenate([-x[:, CH:], x[:, :CH]], axis=1)], axis=0)

    big = real_form(high)
    return jnp.concatenate([big, big, real_form(low)], axis=0)


def product(a, b):
    return jnp.dot(a, b, preferred_element_type=f32)


def weights_kernel(*refs):
    *c_refs, o_ref = refs
    parts = len(c_refs) // 3
    earlier_refs = [entries(c_refs[n * parts : (n + 1) * parts]) for n in range(3)]
    count = o_ref.shape[0]
    bins = range(count)
    f = lax.broadcasted_iota(jnp.int32, (CH, CH), 0)
    g = lax.broadcasted_iota(jnp.int32, (CH, CH), 1)
    eye = (f == g).astype(f32)
    eye2 = jnp.concatenate([eye, jnp.zeros_like(eye)], axis=1)
    segment = lax.axis_index("segment")
    decay = [jnp.where(segment > n, decay_rate**n, 0.0) for n in range(3)]
    a, x, e = [], [], []
    for i in bins:
        terms = [decay[n] * ref[j] for n in range(3) for ref, j in (earlier_refs[n][i],)]
        packed = terms[0] + terms[1] + terms[2]
        flipped = packed.T
        re = jnp.where(f <= g, packed, flipped) + diag_load * eye
        im = jnp.where(f > g, packed, jnp.where(f < g, -flipped, 0.0))
        scale = 1.0 / jnp.sum(jnp.sum(re * eye, axis=1, keepdims=True), axis=0, keepdims=True)
        loaded = jnp.concatenate([re, im], axis=1)
        a.append(right(loaded))
        e.append(eye2 - loaded * scale)
        x.append((eye2 + e[i]) * scale)

    def both(x, e):
        return left(jnp.concatenate([x, e], axis=0))

    for turn in range(NS_STEPS // 3):
        if turn == 0:
            e = [product(left(e[i]), right(e[i])) for i in bins]
        else:
            e = [eye2 - product(left(x[i]), a[i]) for i in bins]
        for _ in range(1 if turn == 0 else 2):
            m = [product(both(x[i], e[i]), right(e[i])) for i in bins]
            x = [x[i] + m[i][:CH] for i in bins]
            e = [m[i][CH:] for i in bins]
        x = [x[i] + product(left(x[i]), right(e[i])) for i in bins]

    c, s = unit_phasor((f * (2 * g - BEAMS)) & (2 * BEAMS - 1), 2 * BEAMS)
    steer = jnp.concatenate([c, s], axis=1) * (1.0 / math.sqrt(CH))
    table = right(steer)
    vec = [product(left(x[i]), table) for i in bins]
    for i in bins:
        inner = steer * vec[i]
        gain = jnp.sum(inner[:, :BEAMS] + inner[:, BEAMS:], axis=0, keepdims=True)
        re = (vec[i][:, :BEAMS] / gain).astype(bf16)
        im = (vec[i][:, BEAMS:] / gain).astype(bf16)
        o_ref[i, :CH, :BEAMS] = re
        o_ref[i, :CH, BEAMS:] = -im
        o_ref[i, CH:, :BEAMS] = im
        o_ref[i, CH:, BEAMS:] = re


def beam_weights(parts):
    count = sum(part.shape[0] for part in parts[0])
    vmem = pl.BlockSpec(memory_space=pltpu.VMEM)
    operands = [part for back in parts for part in back]
    return pl.pallas_call(
        weights_kernel,
        out_shape=jax.ShapeDtypeStruct((count, 2 * CH, 2 * BEAMS), bf16),
        in_specs=[vmem] * len(operands),
        out_specs=vmem,
        compiler_params=params(32),
        name="weights",
    )(*operands)


def earlier(cov):
    if len(cov) == 1:
        c3, c1, c2 = (shifted(cov[0], by) for by in (3, 1, 2))
        return [c1], [c2], [c3]
    low, high = cov
    low1, high3 = shifted(low, 1), shifted(high, 3)
    high1, low3 = shifted(high, 1), shifted(low, 3)
    low2, high2 = shifted(low1, 1), shifted(high3, 3)
    return [low1, high1], [low2, high2], [low3, high3]


def compression_table(code_phase, block_len):
    length = code_phase.shape[0]
    input_pos = jnp.arange(2 * block_len, dtype=jnp.int32)[None, :]
    output_pos = jnp.arange(block_len, dtype=jnp.int32)[:, None]
    lag_index = input_pos - output_pos
    onehot = (lag_index[:, :, None] == jnp.arange(length, dtype=jnp.int32)[None, None, :]).astype(
        jnp.float32
    )
    code_table = jnp.stack([jnp.cos(code_phase), jnp.sin(code_phase)]) / math.sqrt(length)
    table = jnp.einsum("pql,kl->kpq", onehot, code_table, precision=highest)
    return table.astype(bf16).reshape(2 * block_len, 2 * block_len)


def make_compress_kernel(skip):
    def compress_kernel(table_ref, y_hbm, z_out, y_ref, in_sem, *held):
        count, sources, per, _ = y_ref.shape
        z_ref, out_sem = held if held else (z_out, None)
        step = CBLK // per
        half = CH

        def load(i):
            return pltpu.make_async_copy(y_hbm.at[:, skip + i], y_ref.at[i], in_sem.at[i])

        def save(i):
            return pltpu.make_async_copy(z_ref.at[i], z_out.at[i], out_sem.at[i])

        for i in range(count):
            load(i).start()
        for i in range(count):
            load(i).wait()
            for start in range(0, sources, step):
                stop = min(start + 2 * step, sources)
                y = y_ref[i, start:stop].reshape((stop - start) * per, 2 * half)
                m = jnp.dot(table_ref[:, : y.shape[0]], y, preferred_element_type=f32)
                r = pl.ds(start * per, CBLK)
                z_ref[i, r, :half] = (m[:CBLK, :half] + m[CBLK:, half:]).astype(bf16)
                z_ref[i, r, half:] = (m[:CBLK, half:] - m[CBLK:, :half]).astype(bf16)
            if held:
                save(i).start()
        if held:
            for i in range(count):
                save(i).wait()

    return compress_kernel


def compress(owned, table, skip, count, stay):
    sources, _, per, width = owned.shape
    vmem = pl.BlockSpec(memory_space=pltpu.VMEM)
    anywhere = pl.BlockSpec(memory_space=pl.ANY)
    shape = (count, sources * per, width)
    scratch = [
        pltpu.VMEM((count, sources, per, width), bf16),
        pltpu.SemaphoreType.DMA((count,)),
    ]
    if not stay:
        scratch += [pltpu.VMEM(shape, bf16), pltpu.SemaphoreType.DMA((count,))]
    return pl.pallas_call(
        make_compress_kernel(skip),
        out_shape=jax.ShapeDtypeStruct(shape, bf16) if stay else pltpu.HBM(shape, bf16),
        in_specs=[vmem, anywhere],
        out_specs=vmem if stay else anywhere,
        scratch_shapes=scratch,
        compiler_params=params(32),
        name="compress",
    )(table, owned)


def make_beams_kernel(first, skip, parts, aliased):
    def beams_kernel(w_ref, *refs):
        z_in = entries(refs[:parts])
        o_hbm, o_ref, out_sem, *held = refs[parts + aliased :]
        count, rows, _ = o_ref.shape
        pieces = out_sem.shape[1]
        step = rows // pieces

        def load(i):
            ref, j = z_in[skip + i]
            return pltpu.make_async_copy(ref.at[j], held[0].at[i], held[1].at[i])

        def save(i, p):
            r = pl.ds(p * step, step)
            return pltpu.make_async_copy(
                o_ref.at[i, r], o_hbm.at[first + skip + i, r], out_sem.at[i, p]
            )

        if held:
            for i in range(count):
                load(i).start()
        for i in range(count):
            if held:
                load(i).wait()
                source = held[0].at[i]
            else:
                ref, j = z_in[skip + i]
                source = ref.at[j]
            for p in range(pieces):
                r = pl.ds(p * step, step)
                o_ref[i, r] = jnp.dot(
                    source[r], w_ref[skip + i], preferred_element_type=f32
                ).astype(bf16)
                save(i, p).start()
        for i in range(count):
            for p in range(pieces):
                save(i, p).wait()

    return beams_kernel


def form_beams(z, weights, held, bins, first, skip, count, stay):
    rows = z[0].shape[1]
    width = weights.shape[2]
    vmem = pl.BlockSpec(memory_space=pltpu.VMEM)
    anywhere = pl.BlockSpec(memory_space=pl.ANY)
    before = [] if held is None else [held]
    pieces = 2 if stay else 1
    scratch = [
        pltpu.VMEM((count, rows, width), bf16),
        pltpu.SemaphoreType.DMA((count, pieces)),
    ]
    if not stay:
        scratch += [pltpu.VMEM((count, rows, width), bf16), pltpu.SemaphoreType.DMA((count,))]
    return pl.pallas_call(
        make_beams_kernel(first, skip, len(z), len(before)),
        out_shape=jax.ShapeDtypeStruct((bins, rows, width), bf16),
        in_specs=[vmem] + [vmem if stay else anywhere] * len(z) + [anywhere] * len(before),
        out_specs=anywhere,
        scratch_shapes=scratch,
        input_output_aliases={1 + len(z): 0} if before else {},
        compiler_params=params(32 if stay else 60),
        name="beams",
    )(weights, *z, *before)


def chain(echoes, train_blocks, hard_bins, owner_map, code_phase):
    samples = echoes[0]
    blocks, hard = train_blocks[0], hard_bins[0]
    owners = lax.axis_size("blk")
    bins = hard.shape[0]
    firsts = [sum(CHUNKS[:i]) for i in range(len(CHUNKS))]
    spectra = []
    for first, count in zip(firsts, CHUNKS):
        sent = doppler(samples, owner_map, owners, first, count)
        spectra.append(sent.reshape(owners, count, samples.shape[0], 2 * CH))
    code_phase, spectra[0] = lax.optimization_barrier((code_phase, spectra[0]))
    table = compression_table(code_phase, CBLK)
    owned = []
    for g, sent in enumerate(spectra):
        if g > 0:
            sent, owned[-1] = lax.optimization_barrier((sent, owned[-1]))
        owned.append(lax.all_to_all(sent, "blk", split_axis=0, concat_axis=0, tiled=True))
    result = None
    for g, (first, y) in enumerate(zip(firsts, owned)):
        count = y.shape[1]
        last = g == len(CHUNKS) - 1
        pieces = [count] if last else [count // 2, count - count // 2]
        parts = earlier(covariance(y, blocks, hard, first, pieces))
        z = []
        for n, some in enumerate(pieces):
            z.append(compress(y, table, sum(pieces[:n]), some, last))
        weights = beam_weights(parts)
        spans = [(0, count)] if last else [(0, EARLY), (EARLY, count - EARLY)]
        for skip, some in spans:
            result = form_beams(z, weights, result, bins, first, skip, some, last)
    return result[None]


def solution(mesh):
    in_specs = (
        P("segment", "blk", None, None),
        P("segment", "blk", None),
        P("segment", "blk"),
        P(),
        P(),
    )
    out_specs = P("segment", "blk", None, None)
    return jax.shard_map(chain, mesh=mesh, in_specs=in_specs, out_specs=out_specs, check_vma=False)
```

```python
import math

import jax
import jax.numpy as jnp
from jax import lax
from jax.experimental import pallas as pl
from jax.experimental.pallas import tpu as pltpu
from jax.sharding import PartitionSpec as P


CH = 128
BEAMS = 128
RB = 32
NTR_EASY = 3
NS_STEPS = 12
CBLK = 128
CHUNKS = (6, 2)
RESIDENT = 6

decay_rate = 0.7
diag_load = 0.1
highest = lax.Precision.HIGHEST
f32 = jnp.float32
bf16 = jnp.bfloat16
MiB = 1 << 20


def params(limit=48):
    return pltpu.CompilerParams(vmem_limit_bytes=limit * MiB)


def shifted(x, by):
    peers = lax.axis_size("segment")
    return lax.ppermute(x, "segment", [(i, (i + by) % peers) for i in range(peers)])


def unit_phasor(index, period):
    eighth = period // 8
    turned = index + eighth
    quadrant = lax.shift_right_logical(turned, int(math.log2(period // 4))) & 3
    rest = (turned & (period // 4 - 1)) - eighth
    x = rest.astype(f32) * (2.0 * math.pi / period)
    x2 = x * x
    sine = x + x * x2 * (-1.0 / 6 + x2 * (1.0 / 120 + x2 * (-1.0 / 5040 + x2 * (1.0 / 362880))))
    cosine = 1.0 + x2 * (
        -0.5 + x2 * (1.0 / 24 + x2 * (-1.0 / 720 + x2 * (1.0 / 40320 - x2 * (1.0 / 3628800))))
    )
    swap = (quadrant & 1) == 1
    c = jnp.where(swap, sine, cosine)
    s = jnp.where(swap, cosine, sine)
    c = jnp.where((quadrant == 1) | (quadrant == 2), -c, c)
    s = jnp.where(quadrant >= 2, -s, s)
    return c, s


def make_doppler_kernel(owners, first, count):
    def doppler_kernel(map_ref, x_hbm, o_hbm, x_ref, table_ref, rows_ref, o_ref, in_sem, out_sem):
        slots = owners * count
        total = map_ref.shape[1]
        bins = total // owners
        pulses = x_ref.shape[2] // 2
        groups, _, rows, _ = o_ref.shape
        pitch = rows_ref.shape[1] // slots
        loads = in_sem.shape[0]
        per_load = x_ref.shape[0] // loads

        def load(i):
            piece = pl.ds(i * per_load, per_load)
            return pltpu.make_async_copy(x_hbm.at[piece], x_ref.at[piece], in_sem.at[i])

        def save(i):
            piece = o_hbm.at[:, pl.ds(i * rows, rows), :]
            return pltpu.make_async_copy(o_ref.at[i], piece, out_sem.at[i])

        for i in range(loads):
            load(i).start()
        slot = lax.broadcasted_iota(jnp.int32, (slots, total), 1)
        row = lax.broadcasted_iota(jnp.int32, (slots, total), 0)
        place = slot % bins - first
        mine = (place >= 0) & (place < count) & (slot // bins * count + place == row)
        chosen = jnp.sum(jnp.where(mine, map_ref[...].astype(f32), 0.0), axis=1, keepdims=True)
        pulse = lax.broadcasted_iota(jnp.int32, (slots, pulses), 1)
        c, s = unit_phasor((pulse * chosen.astype(jnp.int32)) & (pulses - 1), pulses)
        c = (c * (1.0 / math.sqrt(pulses))).astype(bf16)
        s = (s * (1.0 / math.sqrt(pulses))).astype(bf16)
        table_ref[:slots, :pulses] = c
        table_ref[:slots, pulses:] = s
        table_ref[slots:, :pulses] = -s
        table_ref[slots:, pulses:] = c

        def group(i, carry):
            for j in range(loads // groups):
                load(i * (loads // groups) + j).wait()
            for pair in range(rows // 2):
                x = x_ref[pl.ds(i * rows + 2 * pair, 2)].reshape(2 * CH, 2 * pulses)
                d = lax.dot_general(
                    table_ref[...], x, (((1,), (1,)), ((), ())), preferred_element_type=f32
                )
                for part in range(2):
                    for half in range(2):
                        rows_ref[part, pl.ds(2 * pair + half, slots, stride=pitch), :] = d[
                            part * slots : (part + 1) * slots, half * CH : (half + 1) * CH
                        ]
            for part in range(2):
                o_ref[i, :, :, part * CH : (part + 1) * CH] = (
                    rows_ref[part].reshape(slots, pitch, CH)[:, :rows].astype(bf16)
                )
            save(i).start()
            return carry

        lax.fori_loop(0, groups, group, 0)
        for i in range(groups):
            save(i).wait()

    return doppler_kernel


def doppler(samples, owner_map, owners, first, count):
    range_local, channels, double_pulses = samples.shape
    slots = owners * count
    rows, pitch, loads = 16, 24, 8
    groups = range_local // rows
    return pl.pallas_call(
        make_doppler_kernel(owners, first, count),
        out_shape=pltpu.HBM((slots, range_local, 2 * channels), bf16),
        in_specs=[
            pl.BlockSpec(memory_space=pltpu.VMEM),
            pl.BlockSpec(memory_space=pl.ANY),
        ],
        out_specs=pl.BlockSpec(memory_space=pl.ANY),
        scratch_shapes=[
            pltpu.VMEM(samples.shape, bf16),
            pltpu.VMEM((2 * slots, double_pulses), bf16),
            pltpu.VMEM((2, slots * pitch, channels), f32),
            pltpu.VMEM((groups, slots, rows, 2 * channels), bf16),
            pltpu.SemaphoreType.DMA((loads,)),
            pltpu.SemaphoreType.DMA((groups,)),
        ],
        compiler_params=pltpu.CompilerParams(vmem_limit_bytes=67_043_328),
        name="doppler",
    )(owner_map.reshape(1, -1), samples)


def entries(refs):
    return [(ref, j) for ref in refs for j in range(ref.shape[0])]


def make_cov_kernel(first, count, listed):
    def cov_kernel(blocks_ref, hard_ref, y_ref, *refs):
        *o_refs, buf, sem = refs
        per_source = y_ref.shape[2] // RB

        def copy(i, t):
            block = blocks_ref[first + i, t]
            source = block // per_source
            row = pl.multiple_of((block % per_source) * RB, RB)
            return pltpu.make_async_copy(
                y_ref.at[source, i, pl.ds(row, RB), :], buf.at[i, t], sem.at[i, t]
            )

        for i in range(count):
            for t in range(listed):
                copy(i, t).start()
        row_of = lax.broadcasted_iota(jnp.int32, (listed * RB, 1), 0)
        f = lax.broadcasted_iota(jnp.int32, (CH, CH), 0)
        g = lax.broadcasted_iota(jnp.int32, (CH, CH), 1)
        for i in range(count):
            for t in range(listed):
                copy(i, t).wait()
        used = [
            jnp.where(hard_ref[first + i] == 1, listed * RB, NTR_EASY * RB) for i in range(count)
        ]
        rows = [
            buf[i].reshape(listed * RB, 2 * CH) * (row_of < used[i]).astype(f32).astype(bf16)
            for i in range(count)
        ]
        grams = [
            lax.dot_general(y, y, (((0,), (0,)), ((), ())), preferred_element_type=f32)
            for y in rows
        ]
        for i, (o_ref, j) in enumerate(entries(o_refs)):
            re = grams[i][:CH, :CH] + grams[i][CH:, CH:]
            im = grams[i][CH:, :CH] - grams[i][:CH, CH:]
            o_ref[j] = jnp.where(f <= g, re, im) / used[i].astype(f32)

    return cov_kernel


def covariance(owned, blocks, hard, first, pieces):
    count = owned.shape[1]
    listed = blocks.shape[1]
    smem = pl.BlockSpec(memory_space=pltpu.SMEM)
    return pl.pallas_call(
        make_cov_kernel(first, count, listed),
        out_shape=[jax.ShapeDtypeStruct((n, CH, CH), f32) for n in pieces],
        in_specs=[smem, smem, pl.BlockSpec(memory_space=pltpu.HBM)],
        out_specs=[pl.BlockSpec(memory_space=pltpu.VMEM)] * len(pieces),
        scratch_shapes=[
            pltpu.VMEM((count, listed, RB, 2 * CH), bf16),
            pltpu.SemaphoreType.DMA((count, listed)),
        ],
        compiler_params=params(16),
        name="covariance",
    )(blocks, hard, owned)


def halves(z):
    high = z.astype(bf16)
    return high, (z - high.astype(f32)).astype(bf16)


def left(z):
    high, low = halves(z)
    return jnp.concatenate([high, low, high], axis=1)


def right(z):
    high, low = halves(z)

    def real_form(x):
        return jnp.concatenate([x, jnp.concatenate([-x[:, CH:], x[:, :CH]], axis=1)], axis=0)

    big = real_form(high)
    return jnp.concatenate([big, big, real_form(low)], axis=0)


def product(a, b):
    return jnp.dot(a, b, preferred_element_type=f32)


def weights_kernel(*refs):
    *c_refs, o_ref = refs
    parts = len(c_refs) // 3
    earlier_refs = [entries(c_refs[n * parts : (n + 1) * parts]) for n in range(3)]
    count = o_ref.shape[0]
    bins = range(count)
    f = lax.broadcasted_iota(jnp.int32, (CH, CH), 0)
    g = lax.broadcasted_iota(jnp.int32, (CH, CH), 1)
    eye = (f == g).astype(f32)
    eye2 = jnp.concatenate([eye, jnp.zeros_like(eye)], axis=1)
    segment = lax.axis_index("segment")
    decay = [jnp.where(segment > n, decay_rate**n, 0.0) for n in range(3)]
    a, x, e = [], [], []
    for i in bins:
        terms = [decay[n] * ref[j] for n in range(3) for ref, j in (earlier_refs[n][i],)]
        packed = terms[0] + terms[1] + terms[2]
        flipped = packed.T
        re = jnp.where(f <= g, packed, flipped) + diag_load * eye
        im = jnp.where(f > g, packed, jnp.where(f < g, -flipped, 0.0))
        scale = 1.0 / jnp.sum(jnp.sum(re * eye, axis=1, keepdims=True), axis=0, keepdims=True)
        loaded = jnp.concatenate([re, im], axis=1)
        a.append(right(loaded))
        e.append(eye2 - loaded * scale)
        x.append((eye2 + e[i]) * scale)

    def both(x, e):
        return left(jnp.concatenate([x, e], axis=0))

    for turn in range(NS_STEPS // 3):
        if turn == 0:
            e = [product(left(e[i]), right(e[i])) for i in bins]
        else:
            e = [eye2 - product(left(x[i]), a[i]) for i in bins]
        for _ in range(1 if turn == 0 else 2):
            m = [product(both(x[i], e[i]), right(e[i])) for i in bins]
            x = [x[i] + m[i][:CH] for i in bins]
            e = [m[i][CH:] for i in bins]
        x = [x[i] + product(left(x[i]), right(e[i])) for i in bins]

    c, s = unit_phasor((f * (2 * g - BEAMS)) & (2 * BEAMS - 1), 2 * BEAMS)
    steer = jnp.concatenate([c, s], axis=1) * (1.0 / math.sqrt(CH))
    table = right(steer)
    vec = [product(left(x[i]), table) for i in bins]
    for i in bins:
        inner = steer * vec[i]
        gain = jnp.sum(inner[:, :BEAMS] + inner[:, BEAMS:], axis=0, keepdims=True)
        re = (vec[i][:, :BEAMS] / gain).astype(bf16)
        im = (vec[i][:, BEAMS:] / gain).astype(bf16)
        o_ref[i, :CH, :BEAMS] = re
        o_ref[i, :CH, BEAMS:] = -im
        o_ref[i, CH:, :BEAMS] = im
        o_ref[i, CH:, BEAMS:] = re


def beam_weights(parts):
    count = sum(part.shape[0] for part in parts[0])
    vmem = pl.BlockSpec(memory_space=pltpu.VMEM)
    operands = [part for back in parts for part in back]
    return pl.pallas_call(
        weights_kernel,
        out_shape=jax.ShapeDtypeStruct((count, 2 * CH, 2 * BEAMS), bf16),
        in_specs=[vmem] * len(operands),
        out_specs=vmem,
        compiler_params=params(32),
        name="weights",
    )(*operands)


def earlier(cov):
    if len(cov) == 1:
        c3, c1, c2 = (shifted(cov[0], by) for by in (3, 1, 2))
        return [c1], [c2], [c3]
    low, high = cov
    low1, high3 = shifted(low, 1), shifted(high, 3)
    high1, low3 = shifted(high, 1), shifted(low, 3)
    low2, high2 = shifted(low1, 1), shifted(high3, 3)
    return [low1, high1], [low2, high2], [low3, high3]


def compression_table(code_phase, block_len):
    length = code_phase.shape[0]
    input_pos = jnp.arange(2 * block_len, dtype=jnp.int32)[None, :]
    output_pos = jnp.arange(block_len, dtype=jnp.int32)[:, None]
    lag_index = input_pos - output_pos
    onehot = (lag_index[:, :, None] == jnp.arange(length, dtype=jnp.int32)[None, None, :]).astype(
        jnp.float32
    )
    code_table = jnp.stack([jnp.cos(code_phase), jnp.sin(code_phase)]) / math.sqrt(length)
    table = jnp.einsum("pql,kl->kpq", onehot, code_table, precision=highest)
    return table.astype(bf16).reshape(2 * block_len, 2 * block_len)


def compress_kernel(table_ref, y_hbm, z_out, y_ref, in_sem, *held):
    count, sources, per, _ = y_ref.shape
    z_ref, out_sem = held if held else (z_out, None)
    step = CBLK // per
    half = CH

    def load(i):
        return pltpu.make_async_copy(y_hbm.at[:, i], y_ref.at[i], in_sem.at[i])

    def save(i):
        return pltpu.make_async_copy(z_ref.at[i], z_out.at[i], out_sem.at[i])

    for i in range(count):
        load(i).start()
    for i in range(count):
        load(i).wait()
        for start in range(0, sources, step):
            stop = min(start + 2 * step, sources)
            y = y_ref[i, start:stop].reshape((stop - start) * per, 2 * half)
            m = jnp.dot(table_ref[:, : y.shape[0]], y, preferred_element_type=f32)
            r = pl.ds(start * per, CBLK)
            z_ref[i, r, :half] = (m[:CBLK, :half] + m[CBLK:, half:]).astype(bf16)
            z_ref[i, r, half:] = (m[:CBLK, half:] - m[CBLK:, :half]).astype(bf16)
        if held:
            save(i).start()
    if held:
        for i in range(count):
            save(i).wait()


def compress(owned, table):
    sources, count, per, width = owned.shape
    vmem = pl.BlockSpec(memory_space=pltpu.VMEM)
    anywhere = pl.BlockSpec(memory_space=pl.ANY)
    shape = (count, sources * per, width)
    scratch = [
        pltpu.VMEM((count, sources, per, width), bf16),
        pltpu.SemaphoreType.DMA((count,)),
    ]
    if count > RESIDENT:
        scratch += [pltpu.VMEM(shape, bf16), pltpu.SemaphoreType.DMA((count,))]
    return pl.pallas_call(
        compress_kernel,
        out_shape=pltpu.HBM(shape, bf16) if count > RESIDENT else jax.ShapeDtypeStruct(shape, bf16),
        in_specs=[vmem, anywhere],
        out_specs=anywhere if count > RESIDENT else vmem,
        scratch_shapes=scratch,
        compiler_params=params(32),
        name="compress",
    )(table, owned)


def make_beams_kernel(first, aliased):
    def beams_kernel(w_ref, z_in, *refs):
        o_hbm, o_ref, out_sem, *held = refs[aliased:]
        z_ref, in_sem = held if held else (z_in, None)
        count, rows, _ = z_ref.shape
        pieces = out_sem.shape[1]
        step = rows // pieces

        def load(i):
            return pltpu.make_async_copy(z_in.at[i], z_ref.at[i], in_sem.at[i])

        def save(i, p):
            piece = pl.ds(p * step, step)
            return pltpu.make_async_copy(
                o_ref.at[i, piece], o_hbm.at[first + i, piece], out_sem.at[i, p]
            )

        if held:
            for i in range(count):
                load(i).start()
        for i in range(count):
            if held:
                load(i).wait()
            for p in range(pieces):
                r = pl.ds(p * step, step)
                o_ref[i, r] = jnp.dot(
                    z_ref[i, r], w_ref[i], preferred_element_type=f32
                ).astype(bf16)
                save(i, p).start()
        for i in range(count):
            for p in range(pieces):
                save(i, p).wait()

    return beams_kernel


def form_beams(z, weights, held, bins, first):
    count, rows, _ = z.shape
    width = weights.shape[2]
    resident = count <= RESIDENT
    vmem = pl.BlockSpec(memory_space=pltpu.VMEM)
    anywhere = pl.BlockSpec(memory_space=pl.ANY)
    in_specs = [vmem, vmem if resident else anywhere]
    operands = [weights, z]
    aliases = {}
    if held is not None:
        in_specs.append(anywhere)
        operands.append(held)
        aliases = {2: 0}
    pieces = 2 if resident else 1
    scratch = [
        pltpu.VMEM((count, rows, width), bf16),
        pltpu.SemaphoreType.DMA((count, pieces)),
    ]
    if not resident:
        scratch += [pltpu.VMEM(z.shape, bf16), pltpu.SemaphoreType.DMA((count,))]
    return pl.pallas_call(
        make_beams_kernel(first, len(aliases)),
        out_shape=jax.ShapeDtypeStruct((bins, rows, width), bf16),
        in_specs=in_specs,
        out_specs=anywhere,
        scratch_shapes=scratch,
        input_output_aliases=aliases,
        compiler_params=params(32 if resident else 59),
        name="beams",
    )(*operands)


def chain(echoes, train_blocks, hard_bins, owner_map, code_phase):
    samples = echoes[0]
    blocks, hard = train_blocks[0], hard_bins[0]
    owners = lax.axis_size("blk")
    bins = hard.shape[0]
    firsts = [sum(CHUNKS[:i]) for i in range(len(CHUNKS))]
    spectra = []
    for first, count in zip(firsts, CHUNKS):
        sent = doppler(samples, owner_map, owners, first, count)
        spectra.append(sent.reshape(owners, count, samples.shape[0], 2 * CH))
    code_phase, spectra[0] = lax.optimization_barrier((code_phase, spectra[0]))
    table = compression_table(code_phase, CBLK)
    owned = []
    for g, sent in enumerate(spectra):
        if g > 0:
            sent, owned[-1] = lax.optimization_barrier((sent, owned[-1]))
        owned.append(lax.all_to_all(sent, "blk", split_axis=0, concat_axis=0, tiled=True))
    result = None
    for first, y in zip(firsts, owned):
        count = y.shape[1]
        pieces = [count // 2, count - count // 2] if count > 3 else [count]
        parts = earlier(covariance(y, blocks, hard, first, pieces))
        z = compress(y, table)
        weights = beam_weights(parts)
        result = form_beams(z, weights, result, bins, first)
    return result[None]


def solution(mesh):
    in_specs = (
        P("segment", "blk", None, None),
        P("segment", "blk", None),
        P("segment", "blk"),
        P(),
        P(),
    )
    out_specs = P("segment", "blk", None, None)
    return jax.shard_map(chain, mesh=mesh, in_specs=in_specs, out_specs=out_specs, check_vma=False)
```
